512 devices in a mesh: fsdp: 32 (over y, x_hi, core), tensor: 16 (over x_lo, z).
Axes of the slice: x: 4 (x_hi: 2, x_lo: 2; x = x_hi * 2 + x_lo), y: 8, z: 8, core: 2. Of those that a mesh axis runs over, the one named last changes fastest.
Arguments:
- out_grad: bfloat16 [4096, 8192], P(('fsdp', 'tensor')), may hold values from -24 to 24
- live_rows: int32 [512], P(('fsdp', 'tensor')), may hold values from 1 to 8, as said below
- gate_pre: bfloat16 [4096, 12288], P('fsdp', 'tensor'), may hold values from -8 to 8
- up_pre: bfloat16 [4096, 12288], P('fsdp', 'tensor'), may hold values from -6 to 6
- down_weight: bfloat16 [12288, 8192], P('tensor', 'fsdp'), may hold values from -0.15625 to 0.15625
- tile_mask: int32 [96, 64], P('tensor'), may hold values from 0 to 1, as said below
Outputs:
- d_gate: bfloat16 [4096, 12288], P('fsdp', 'tensor')
- d_up: bfloat16 [4096, 12288], P('fsdp', 'tensor')
- d_weight: bfloat16 [12288, 8192], P('tensor', 'fsdp')
The draws below stay inside these ranges and needn't reach their ends.
Inputs may be any that keep to these rules, and one draw needn't show every extreme that they name: `tile_mask`: each device's shard of 6 x 2 tiles holds 1 to 4 kept tiles; in every draw the shards of some tensor index all hold exactly 4, and every tensor index has a shard holding 4. `live_rows`: some device has all 8 rows live in every draw.
All inputs are finite; a program needn't handle non-finite values.
Results may differ from the reference program's by a relative error of at most 0.015.
Values may be sent and summed in bfloat16 or wider, within the bound.
No kernel may reach another device: no remote copies, remote signals or barrier semaphores. Data moves between devices by JAX's collectives and lax.ppermute only.
A program may use at most 64 MiB of HBM per device.

```python
import math
import jax
import jax.numpy as jnp
from jax import lax

D = 8192
FF = 12288
BLK = 128
CAP = 4
TOK_DEV = 8
ROWS = 128
TOKENS = 4096
FB = 96
DB = 64
ROWB = 6
COLB = 2
N_FSDP = 32


def draw_tile_mask(key, part):
    tensor_count = FB // ROWB
    fsdp_count = DB // COLB
    local_count = ROWB * COLB
    key_one, key_two, key_three, key_four = jax.random.split(jax.random.fold_in(key, 11), 4)
    counts = jax.random.randint(key_one, (tensor_count, fsdp_count), 1, CAP + 1)
    full_row = jax.random.randint(key_two, (), 0, tensor_count)
    full_col = jax.random.randint(key_three, (tensor_count,), 0, fsdp_count)
    tensor_ids = jnp.arange(tensor_count)[:, None]
    fsdp_ids = jnp.arange(fsdp_count)[None, :]
    counts = jnp.where((tensor_ids == full_row) | (fsdp_ids == full_col[:, None]), CAP, counts)
    scores = jax.random.randint(key_four, (tensor_count, fsdp_count, local_count), 0, 1 << 20) * local_count + jnp.arange(local_count)
    order = jnp.argsort(scores, axis=-1)
    ranks = jnp.argsort(order, axis=-1)
    chosen = (ranks < counts[:, :, None]).astype(jnp.int32)
    chosen = chosen.reshape(tensor_count, fsdp_count, ROWB, COLB).transpose(0, 2, 1, 3)
    return chosen.reshape(tensor_count * ROWB, fsdp_count * COLB)


def draw_live_rows(key, part):
    device_count = TOKENS // TOK_DEV
    key_one, key_two = jax.random.split(jax.random.fold_in(key, 23))
    counts = jax.random.randint(key_one, (device_count,), 1, TOK_DEV + 1)
    full_device = jax.random.randint(key_two, (), 0, device_count)
    return jnp.where(jnp.arange(device_count) == full_device, TOK_DEV, counts).astype(jnp.int32)


def spiked(drawn, own_key, source, target, blocks, factor):
    owner, partner = [(jnp.arange(drawn.shape[axis_at]) // (drawn.shape[axis_at] // blocks)).reshape([-1 if axis == axis_at else 1 for axis in range(drawn.ndim)]) for axis_at in (source, target)]
    chosen = jax.random.permutation(own_key, blocks)[partner]
    strong = (owner == chosen) | (owner == (partner + blocks // 2) % blocks)
    return jnp.where(strong, factor * drawn, drawn)


def shard_levels(own_key, extent, pieces, least, largest):
    level = 1.0
    for axis_at, shards_of in pieces:
        heights = jax.random.uniform(jax.random.fold_in(jax.random.fold_in(own_key, 6), axis_at), (shards_of,), jnp.float32, least / len(pieces), largest / len(pieces))
        level = level * jnp.repeat(jnp.exp(heights), extent[axis_at] // shards_of).reshape((-1,) + (1,) * (len(extent) - 1 - axis_at))
    return level


def scatter_about(stream_key, extent, spread, bound, pieces=(), held_as=jnp.bfloat16):
    drawn = jax.random.normal(stream_key, extent, jnp.float32) * spread
    if len(pieces) > 0:
        drawn = shard_levels(stream_key, extent, pieces, -0.22, 0.18) * drawn
    return jnp.clip(drawn, min=-bound, max=bound).astype(held_as)


def bell_draw_with(stream_key, extent, spread, limit, pieces, heavy, kind=jnp.bfloat16):
    values = spread * jax.random.normal(stream_key, extent, jnp.float32)
    if pieces:
        values = values * shard_levels(stream_key, extent, pieces, -0.22, 0.18)
    return jnp.clip(spiked(values, jax.random.fold_in(stream_key, 3), *heavy), -limit, limit).astype(kind)


def setup_inputs(seed: int = 0) -> dict:
    key_list = jax.random.split(jax.random.key(seed), 7)
    return {
        "out_grad": bell_draw_with(key_list[0], (TOKENS, D), 1.0, 24.0, ((0, 512),), (0, 1, 512, 6.0)),
        "live_rows": draw_live_rows(jax.random.fold_in(key_list[6], 71), 0),
        "gate_pre": scatter_about(key_list[2], (TOKENS, FF), 1.5, 8.0, ((0, 32), (1, 16))),
        "up_pre": scatter_about(key_list[3], (TOKENS, FF), 1.0, 6.0, ((0, 32), (1, 16))),
        "down_weight": scatter_about(key_list[4], (FF, D), (D // 5) ** -0.5, 0.15625, ((0, 16), (1, 32))),
        "tile_mask": draw_tile_mask(jax.random.fold_in(key_list[6], 71), 0),
    }


def reference(out_grad, live_rows, gate_pre, up_pre, down_weight, tile_mask):
    live_mask = jnp.arange(TOK_DEV, dtype=jnp.int32)[None, :] < live_rows[:, None]
    masked_grad = jnp.where(live_mask.reshape(TOKENS, 1), out_grad, jnp.zeros_like(out_grad))
    tile_gate = tile_mask.astype(jnp.bfloat16)[:, None, :, None]
    masked_weight = (down_weight.reshape(FB, BLK, DB, BLK) * tile_gate).reshape(FF, D)
    d_hidden = jnp.dot(masked_grad, masked_weight.T, preferred_element_type=jnp.float32)
    gate_value = gate_pre.astype(jnp.float32)
    up_value = up_pre.astype(jnp.float32)
    sigmoid_gate = jax.nn.sigmoid(gate_value)
    hidden = (gate_value * sigmoid_gate * up_value).astype(jnp.bfloat16)
    d_up = (d_hidden * gate_value * sigmoid_gate).astype(jnp.bfloat16)
    d_gate = (d_hidden * up_value * sigmoid_gate * (1.0 + gate_value * (1.0 - sigmoid_gate))).astype(jnp.bfloat16)
    grad_scale = 1.0 / math.sqrt(TOKENS)
    mask_float = tile_mask.astype(jnp.float32)[:, None, :, None]

    def add_group(running, group_pair):
        hidden_group, grad_group = group_pair
        partial_sum = jnp.dot(hidden_group.T, grad_group, preferred_element_type=jnp.float32) * grad_scale
        partial_sum = (partial_sum.reshape(FB, BLK, DB, BLK) * mask_float).reshape(FF, D)
        rounded = lax.optimization_barrier(partial_sum.astype(jnp.bfloat16))
        return (running + rounded.astype(jnp.float32), None)
    running, _ = lax.scan(add_group, jnp.zeros((FF, D), jnp.float32), (hidden.reshape(N_FSDP, ROWS, FF), masked_grad.reshape(N_FSDP, ROWS, D)))
    return (d_gate, d_up, running.astype(jnp.bfloat16))
```

```python
import math

import jax
import jax.numpy as jnp
from jax import lax
from jax.experimental import pallas as pl
from jax.experimental.pallas import tpu as pltpu
from jax.sharding import PartitionSpec as P

BLK = 128
CAP = 4
TAB = 8


VMEM = pl.BlockSpec(memory_space=pltpu.VMEM)
SMEM = pl.BlockSpec(memory_space=pltpu.SMEM)


def prep_kernel(f_ref, live_ref, mask_ref, grad_ref, weight_ref, masked_ref, packed_ref):
    row_blocks = mask_ref.shape[0]
    rows = lax.broadcasted_iota(jnp.int32, grad_ref.shape, 0)
    value = grad_ref[...].astype(jnp.float32)
    masked_ref[...] = jnp.where(rows < live_ref[0], value, 0.0).astype(jnp.bfloat16)
    packed_ref[...] = jnp.zeros_like(packed_ref)
    count = jnp.int32(0)
    for r in range(row_blocks):
        for c in range(2):
            kept = mask_ref[r, 2 * f_ref[0] + c]

            @pl.when(kept == 1)
            def _(r=r, c=c, count=count):
                packed_ref[count] = weight_ref[
                    r * BLK : (r + 1) * BLK, c * BLK : (c + 1) * BLK
                ]

            count = count + kept


def table_kernel(f_ref, mask_ref, gate_ref, up_ref, table_ref, hidden_ref):
    row_blocks = mask_ref.shape[0]
    core = lax.rem(f_ref[0], 2)

    def one_shard(s, carry):
        f = 2 * s + core
        base = s * TAB
        for k in range(TAB):
            table_ref[base + k] = 0
        count = jnp.int32(0)
        for r in range(row_blocks):
            for c in range(2):
                table_ref[base + count] = 2 * r + c
                count = count + mask_ref[r, 2 * f + c]
        return carry

    lax.fori_loop(0, table_ref.shape[0] // TAB, one_shard, 0)
    gate = gate_ref[...].astype(jnp.float32)
    up = up_ref[...].astype(jnp.float32)
    hidden = gate * jax.nn.sigmoid(gate) * up
    hidden_ref[...] = hidden.T.astype(jnp.bfloat16)


def partial_kernel(scale, shard_ref, table_ref, own_h, other_h, own_p, other_p, out_ref):
    s = shard_ref[pl.program_id(0)]
    for k in range(CAP):
        b = table_ref[s * TAB + k]
        r = pl.multiple_of((b // 2) * BLK, BLK)
        c = pl.multiple_of((b % 2) * BLK, BLK)
        left = jnp.concatenate(
            [own_h[pl.ds(r, BLK), :], other_h[pl.ds(r, BLK), :]], axis=1
        )
        right = jnp.concatenate(
            [own_p[:, pl.ds(c, BLK)], other_p[:, pl.ds(c, BLK)]], axis=0
        )
        term = jnp.dot(left, right, preferred_element_type=jnp.float32) * scale
        out_ref[0, k] = term.astype(jnp.bfloat16)


def hidden_grad_kernel(f_ref, table_ref, own_p, other_p, weight_ref, out_ref):
    core = lax.rem(f_ref[0], 2)
    out_ref[...] = jnp.zeros_like(out_ref)

    def one_shard(s, carry):
        f = 2 * s + core
        for k in range(CAP):
            b = table_ref[s * TAB + k]
            r = pl.multiple_of((b // 2) * BLK, BLK)
            c = pl.multiple_of((2 * f + b % 2) * BLK, BLK)
            left = jnp.concatenate(
                [own_p[:, pl.ds(c, BLK)], other_p[:, pl.ds(c, BLK)]], axis=0
            )
            term = lax.dot_general(
                left,
                weight_ref[s, k],
                (((1,), (1,)), ((), ())),
                preferred_element_type=jnp.float32,
            )
            rows = own_p.shape[0]
            out_ref[0, :, pl.ds(r, BLK)] += term[:rows]
            out_ref[1, :, pl.ds(r, BLK)] += term[rows:]
        return carry

    lax.fori_loop(0, weight_ref.shape[0], one_shard, 0)


def gates_kernel(own_ref, other_ref, gate_ref, up_ref, d_gate_ref, d_up_ref):
    d_hidden = own_ref[...] + other_ref[...]
    gate = gate_ref[...].astype(jnp.float32)
    up = up_ref[...].astype(jnp.float32)
    s = jax.nn.sigmoid(gate)
    d_up_ref[...] = (d_hidden * gate * s).astype(jnp.bfloat16)
    d_gate_ref[...] = (d_hidden * up * s * (1.0 + gate * (1.0 - s))).astype(jnp.bfloat16)


def place_kernel(f_ref, mask_ref, own_ref, other_ref, out_ref):
    row_blocks = mask_ref.shape[0]
    out_ref[...] = jnp.zeros_like(out_ref)
    count = jnp.int32(0)
    for r in range(row_blocks):
        for c in range(2):
            kept = mask_ref[r, 2 * f_ref[0] + c]

            @pl.when(kept == 1)
            def _(r=r, c=c, count=count):
                total = own_ref[count] + other_ref[count].astype(jnp.float32)
                out_ref[r * BLK : (r + 1) * BLK, c * BLK : (c + 1) * BLK] = total.astype(
                    jnp.bfloat16
                )

            count = count + kept


def shape(dims, dtype=jnp.bfloat16):
    return jax.ShapeDtypeStruct(dims, dtype)


def cost(flops, size):
    return pl.CostEstimate(flops=flops, bytes_accessed=size, transcendentals=0)


def per_device(out_grad, live_rows, gate_pre, up_pre, down_weight, tile_mask):
    fsdp_count = lax.axis_size("fsdp")
    tensor_count = lax.axis_size("tensor")
    f = lax.axis_index("fsdp")
    t = lax.axis_index("tensor")
    ring_y = fsdp_count // 4
    ring_z = tensor_count // 2
    y, xh = f >> 2, (f >> 1) & 1
    xl, z = t >> (ring_z.bit_length() - 1), t & (ring_z - 1)
    tok, width = out_grad.shape
    rows, units = gate_pre.shape
    scale = 1.0 / math.sqrt(rows * fsdp_count)
    f_arr = f.reshape(1).astype(jnp.int32)

    def over_f(x, move):
        return lax.ppermute(x, "fsdp", [(i, move(i)) for i in range(fsdp_count)])

    def over_t(x, move):
        return lax.ppermute(x, "tensor", [(i, move(i)) for i in range(tensor_count)])

    def y_step(x, d):
        return over_f(x, lambda i: (i + 4 * d) % fsdp_count)

    def z_step(x, d):
        return over_t(x, lambda i: (i // ring_z) * ring_z + (i + d) % ring_z)

    def swap_core(x):
        return over_f(x, lambda i: i ^ 1)

    def swap_xh(x):
        return over_f(x, lambda i: i ^ 2)

    def swap_xl(x):
        return over_t(x, lambda i: (i + ring_z) % tensor_count)

    masked, packed = pl.pallas_call(
        prep_kernel,
        out_shape=(shape((tok, width)), shape((CAP, BLK, BLK))),
        in_specs=[SMEM, SMEM, SMEM, VMEM, VMEM],
        out_specs=(VMEM, VMEM),
        name="prep",
        cost_estimate=cost(1000, 1 << 20),
    )(f_arr, live_rows, tile_mask, out_grad, down_weight)

    masked_other = swap_xl(masked)
    packed_other = swap_xh(packed)

    shard_count = fsdp_count // 2
    table, hidden_t = pl.pallas_call(
        table_kernel,
        out_shape=(shape((shard_count * TAB,), jnp.int32), shape((units, rows))),
        in_specs=[SMEM, SMEM, VMEM, VMEM],
        out_specs=(SMEM, VMEM),
        name="hidden",
        cost_estimate=cost(1000, 1 << 20),
    )(f_arr, tile_mask, gate_pre, up_pre)
    hidden_other = swap_core(hidden_t)

    def pair(own, other, index):
        first = jnp.where(index == 0, own, other)
        second = jnp.where(index == 0, other, own)
        return jnp.stack([first, second])

    def gather(block, step, index, count):
        full = jnp.zeros((2, count) + block.shape[1:], block.dtype)

        def put(full, piece, half, at):
            start = (half, at & (count - 1)) + (0,) * (block.ndim - 1)
            return lax.dynamic_update_slice(full, piece[:, None], start)

        full = put(full, block, 0, index)
        up = down = block
        for d in range(1, count // 2):
            up = step(up, 1)
            down = step(down, -1)
            full = put(full, up, 0, index - d + count)
            full = put(full, down, 0, index + d)
        up = step(up[:1], 1)
        down = step(down[1:], -1)
        full = put(full, up, 0, index + count // 2)
        full = put(full, down, 1, index + count // 2)
        return full

    panel = gather(pair(masked, masked_other, xl), z_step, z, ring_z).reshape(rows, width)
    weights = gather(pair(packed, packed_other, xh), y_step, y, ring_y)
    weights = weights.transpose(1, 0, 2, 3, 4).reshape(shard_count, CAP, BLK, BLK)
    panel_other = swap_core(panel)

    def partials(shards):
        count = shards.shape[0]
        wide = 2 * BLK
        core = f & 1
        panel_spec = pl.BlockSpec((rows, wide), lambda i, s, tab, fr: (0, 2 * s[i] + fr[0]))
        whole = pl.BlockSpec((units, rows), lambda i, s, tab, fr: (0, 0))

        def body(shard_ref, table_ref, core_ref, *refs):
            partial_kernel(scale, shard_ref, table_ref, *refs)

        return pl.pallas_call(
            body,
            out_shape=shape((count, CAP, BLK, BLK)),
            grid_spec=pltpu.PrefetchScalarGridSpec(
                num_scalar_prefetch=3,
                grid=(count,),
                in_specs=[whole, whole, panel_spec, panel_spec],
                out_specs=pl.BlockSpec((1, CAP, BLK, BLK), lambda i, s, tab, fr: (i, 0, 0, 0)),
            ),
            name="partial",
            cost_estimate=cost(count * CAP * 2 * BLK * BLK * 2 * rows, count << 18),
        )(
            shards.astype(jnp.int32),
            table,
            core.reshape(1).astype(jnp.int32),
            hidden_t,
            hidden_other,
            panel,
            panel_other,
        )

    def shards_at(*offsets):
        return jnp.concatenate(
            [2 * ((y + d + ring_y) & (ring_y - 1)) + jnp.arange(2) for d in offsets]
        )

    half = ring_y // 2
    far = partials(shards_at(half))
    up, down = y_step(far[:1], 1), y_step(far[1:], -1)
    wide = jnp.float32
    for d in range(half - 1, 0, -1):
        part = partials(shards_at(d, -d))
        part_up, part_down = part[:2], part[2:]
        if d == half - 1:
            send_up = jnp.concatenate(
                [(part_up[:1].astype(wide) + up.astype(wide)).astype(jnp.bfloat16), part_up[1:]]
            )
            send_down = jnp.concatenate(
                [
                    part_down[:1],
                    (part_down[1:].astype(wide) + down.astype(wide)).astype(jnp.bfloat16),
                ]
            )
        else:
            send_up = (part_up.astype(wide) + up.astype(wide)).astype(jnp.bfloat16)
            send_down = (part_down.astype(wide) + down.astype(wide)).astype(jnp.bfloat16)
        up, down = y_step(send_up, 1), y_step(send_down, -1)
    here = partials(shards_at(0)).astype(wide) + up.astype(wide) + down.astype(wide)
    own_sum = lax.dynamic_index_in_dim(here, xh, 0, keepdims=False)
    send_sum = lax.dynamic_index_in_dim(here, 1 - xh, 0, keepdims=False).astype(jnp.bfloat16)
    other_sum = swap_xh(send_sum)

    d_hidden = pl.pallas_call(
        hidden_grad_kernel,
        out_shape=shape((2, rows, units), jnp.float32),
        in_specs=[SMEM, SMEM, VMEM, VMEM, VMEM],
        out_specs=VMEM,
        name="hidden_grad",
        cost_estimate=cost(shard_count * CAP * 4 * rows * BLK * BLK, 6 << 20),
    )(f_arr, table, panel, panel_other, weights)
    other_part = swap_core(d_hidden[1])
    d_gate, d_up = pl.pallas_call(
        gates_kernel,
        out_shape=(shape((rows, units)), shape((rows, units))),
        in_specs=[VMEM] * 4,
        out_specs=(VMEM, VMEM),
        name="gates",
        cost_estimate=cost(1000, 3 << 19),
    )(d_hidden[0], other_part, gate_pre, up_pre)

    d_weight = pl.pallas_call(
        place_kernel,
        out_shape=shape(down_weight.shape),
        in_specs=[SMEM, SMEM, VMEM, VMEM],
        out_specs=VMEM,
        name="place",
        cost_estimate=cost(1000, 1 << 20),
    )(f_arr, tile_mask, own_sum, other_sum)
    return (d_gate, d_up, d_weight)


def solution(mesh):
    return jax.shard_map(
        per_device,
        mesh=mesh,
        in_specs=(
            P(("fsdp", "tensor"), None),
            P(("fsdp", "tensor")),
            P("fsdp", "tensor"),
            P("fsdp", "tensor"),
            P("tensor", "fsdp"),
            P("tensor", None),
        ),
        out_specs=(P("fsdp", "tensor"), P("fsdp", "tensor"), P("tensor", "fsdp")),
        check_vma=False,
    )
```

```python
import math

import jax
import jax.numpy as jnp
from jax import lax
from jax.experimental import pallas as pl
from jax.experimental.pallas import tpu as pltpu
from jax.sharding import PartitionSpec as P


BLK = 128
CAP = 4
TAB = 8


VMEM = pl.BlockSpec(memory_space=pltpu.VMEM)
SMEM = pl.BlockSpec(memory_space=pltpu.SMEM)


def prep_kernel(f_ref, live_ref, mask_ref, grad_ref, weight_ref, masked_ref, packed_ref):
    row_blocks = mask_ref.shape[0]
    rows = lax.broadcasted_iota(jnp.int32, grad_ref.shape, 0)
    value = grad_ref[...].astype(jnp.float32)
    masked_ref[...] = jnp.where(rows < live_ref[0], value, 0.0).astype(jnp.bfloat16)
    packed_ref[...] = jnp.zeros_like(packed_ref)
    count = jnp.int32(0)
    for r in range(row_blocks):
        for c in range(2):
            kept = mask_ref[r, 2 * f_ref[0] + c]

            @pl.when(kept == 1)
            def _(r=r, c=c, count=count):
                packed_ref[count] = weight_ref[
                    r * BLK : (r + 1) * BLK, c * BLK : (c + 1) * BLK
                ]

            count = count + kept


def table_kernel(f_ref, mask_ref, gate_ref, up_ref, table_ref, hidden_ref):
    row_blocks = mask_ref.shape[0]
    core = lax.rem(f_ref[0], 2)

    def one_shard(s, carry):
        f = 2 * s + core
        base = s * TAB
        for k in range(TAB):
            table_ref[base + k] = 0
        count = jnp.int32(0)
        for r in range(row_blocks):
            for c in range(2):
                table_ref[base + count] = 2 * r + c
                count = count + mask_ref[r, 2 * f + c]
        return carry

    lax.fori_loop(0, table_ref.shape[0] // TAB, one_shard, 0)
    gate = gate_ref[...].astype(jnp.float32)
    up = up_ref[...].astype(jnp.float32)
    hidden = gate * jax.nn.sigmoid(gate) * up
    hidden_ref[...] = hidden.T.astype(jnp.bfloat16)


def partial_kernel(scale, dest_ref, table_ref, core_ref, own_h, other_h, own_p, other_p, out_ref):
    dest = dest_ref[pl.program_id(0)]
    wide = 2 * BLK
    for xh in range(2):
        s = 2 * dest + xh
        at = pl.multiple_of((2 * xh + core_ref[0]) * wide, wide)
        right = jnp.concatenate([own_p[:, pl.ds(at, wide)], other_p[:, pl.ds(at, wide)]], axis=0)
        places = [table_ref[s * TAB + k] for k in range(CAP)]
        rows = [pl.multiple_of((b >> 1) * BLK, BLK) for b in places]
        left = jnp.concatenate(
            [
                jnp.concatenate([own_h[pl.ds(r, BLK), :], other_h[pl.ds(r, BLK), :]], axis=1)
                for r in rows
            ],
            axis=0,
        )
        term = jnp.dot(left, right, preferred_element_type=jnp.float32) * scale
        for k, b in enumerate(places):
            tile = term[k * BLK : (k + 1) * BLK]
            kept = jnp.where((b & 1) == 0, tile[:, :BLK], tile[:, BLK:])
            out_ref[0, xh, k] = kept.astype(jnp.bfloat16)


def hidden_grad_kernel(
    table_ref, core_ref, own_p, other_p, weight_ref, own_ref, other_ref
):
    group = pl.program_id(0)
    shards = weight_ref.shape[0]
    wide = 2 * BLK
    rows = own_p.shape[0]

    @pl.when(group == 0)
    def _():
        own_ref[...] = jnp.zeros_like(own_ref)
        other_ref[...] = jnp.zeros_like(other_ref)

    for i in range(shards):
        s = group * shards + i
        at = pl.multiple_of((2 * i + core_ref[0]) * wide, wide)
        left = jnp.concatenate([own_p[:, pl.ds(at, wide)], other_p[:, pl.ds(at, wide)]], axis=0)
        places = [table_ref[s * TAB + k] for k in range(CAP)]
        halves = []
        for k, b in enumerate(places):
            tile = weight_ref[i, k].astype(jnp.float32)
            second = (b & 1) == 1
            zero = jnp.zeros_like(tile)
            halves.append(
                jnp.concatenate(
                    [jnp.where(second, zero, tile), jnp.where(second, tile, zero)], axis=1
                ).astype(jnp.bfloat16)
            )
        term = lax.dot_general(
            left,
            jnp.concatenate(halves, axis=0),
            (((1,), (1,)), ((), ())),
            preferred_element_type=jnp.float32,
        )
        for k, b in enumerate(places):
            r = pl.multiple_of((b >> 1) * BLK, BLK)
            part = term[:, k * BLK : (k + 1) * BLK]
            own_ref[:, pl.ds(r, BLK)] += part[:rows]
            other_ref[:, pl.ds(r, BLK)] += part[rows:]


def combine_kernel(xh_ref, part_ref, up_ref, down_ref, own_ref, send_ref):
    def total(i):
        return (
            part_ref[0, i].astype(jnp.float32)
            + up_ref[i].astype(jnp.float32)
            + down_ref[i].astype(jnp.float32)
        )

    own_ref[...] = total(xh_ref[0])
    send_ref[...] = total(1 - xh_ref[0]).astype(jnp.bfloat16)


def gates_kernel(own_ref, other_ref, gate_ref, up_ref, d_gate_ref, d_up_ref):
    d_hidden = own_ref[...] + other_ref[...]
    gate = gate_ref[...].astype(jnp.float32)
    up = up_ref[...].astype(jnp.float32)
    s = jax.nn.sigmoid(gate)
    d_up_ref[...] = (d_hidden * gate * s).astype(jnp.bfloat16)
    d_gate_ref[...] = (d_hidden * up * s * (1.0 + gate * (1.0 - s))).astype(jnp.bfloat16)


def place_kernel(f_ref, mask_ref, own_ref, other_ref, out_ref):
    row_blocks = mask_ref.shape[0]
    out_ref[...] = jnp.zeros_like(out_ref)
    count = jnp.int32(0)
    for r in range(row_blocks):
        for c in range(2):
            kept = mask_ref[r, 2 * f_ref[0] + c]

            @pl.when(kept == 1)
            def _(r=r, c=c, count=count):
                total = own_ref[count] + other_ref[count].astype(jnp.float32)
                out_ref[r * BLK : (r + 1) * BLK, c * BLK : (c + 1) * BLK] = total.astype(
                    jnp.bfloat16
                )

            count = count + kept


def shape(dims, dtype=jnp.bfloat16):
    return jax.ShapeDtypeStruct(dims, dtype)


def cost(flops, size):
    return pl.CostEstimate(flops=flops, bytes_accessed=size, transcendentals=0)


def per_device(out_grad, live_rows, gate_pre, up_pre, down_weight, tile_mask):
    fsdp_count = lax.axis_size("fsdp")
    tensor_count = lax.axis_size("tensor")
    f = lax.axis_index("fsdp")
    t = lax.axis_index("tensor")
    ring_y = fsdp_count // 4
    ring_z = tensor_count // 2
    y, xh = f >> 2, (f >> 1) & 1
    xl, z = t >> (ring_z.bit_length() - 1), t & (ring_z - 1)
    tok, width = out_grad.shape
    rows, units = gate_pre.shape
    scale = 1.0 / math.sqrt(rows * fsdp_count)
    f_arr = f.reshape(1).astype(jnp.int32)

    def over_f(x, move):
        return lax.ppermute(x, "fsdp", [(i, move(i)) for i in range(fsdp_count)])

    def over_t(x, move):
        return lax.ppermute(x, "tensor", [(i, move(i)) for i in range(tensor_count)])

    def y_step(x, d):
        return over_f(x, lambda i: (i + 4 * d) % fsdp_count)

    def z_step(x, d):
        return over_t(x, lambda i: (i // ring_z) * ring_z + (i + d) % ring_z)

    def swap_core(x):
        return over_f(x, lambda i: i ^ 1)

    def swap_xh(x):
        return over_f(x, lambda i: i ^ 2)

    def swap_xl(x):
        return over_t(x, lambda i: (i + ring_z) % tensor_count)

    masked, packed = pl.pallas_call(
        prep_kernel,
        out_shape=(shape((tok, width)), shape((CAP, BLK, BLK))),
        in_specs=[SMEM, SMEM, SMEM, VMEM, VMEM],
        out_specs=(VMEM, VMEM),
        name="prep",
        cost_estimate=cost(1000, 1 << 20),
    )(f_arr, live_rows, tile_mask, out_grad, down_weight)
    masked_other = swap_xl(masked)
    packed_other = swap_xh(packed)

    shard_count = fsdp_count // 2
    table, hidden_t = pl.pallas_call(
        table_kernel,
        out_shape=(shape((shard_count * TAB,), jnp.int32), shape((units, rows))),
        in_specs=[SMEM, SMEM, VMEM, VMEM],
        out_specs=(SMEM, VMEM),
        name="hidden",
        cost_estimate=cost(1000, 1 << 20),
    )(f_arr, tile_mask, gate_pre, up_pre)
    hidden_other = swap_core(hidden_t)

    def pair(own, other, index):
        first = jnp.where(index == 0, own, other)
        second = jnp.where(index == 0, other, own)
        return jnp.stack([first, second])

    def gather(block, step, index, count):
        full = jnp.zeros((2, count) + block.shape[1:], block.dtype)

        def put(full, piece, at):
            start = (0, at & (count - 1)) + (0,) * (block.ndim - 1)
            return lax.dynamic_update_slice(full, piece[:, None], start)

        full = put(full, block, index)
        up = down = block
        for d in range(1, count // 2 + 1):
            up = step(up, 1)
            full = put(full, up, index - d + count)
            if d < count // 2:
                down = step(down, -1)
                full = put(full, down, index + d)
        return full

    panel = gather(pair(masked, masked_other, xl), z_step, z, ring_z).reshape(rows, width)
    weights = gather(pair(packed, packed_other, xh), y_step, y, ring_y)
    weights = weights.transpose(1, 0, 2, 3, 4).reshape(shard_count, CAP, BLK, BLK)
    panel_other = swap_core(panel)
    core_arr = (f & 1).reshape(1).astype(jnp.int32)

    def partials(*offsets):
        count = len(offsets)
        dests = jnp.stack([(y + d + ring_y) & (ring_y - 1) for d in offsets]).astype(jnp.int32)
        panel_spec = pl.BlockSpec((rows, width // ring_y), lambda i, ds, tab, cr: (0, ds[i]))
        whole = pl.BlockSpec((units, rows), lambda i, ds, tab, cr: (0, 0))

        def body(*refs):
            partial_kernel(scale, *refs)

        return pl.pallas_call(
            body,
            out_shape=shape((count, 2, CAP, BLK, BLK)),
            grid_spec=pltpu.PrefetchScalarGridSpec(
                num_scalar_prefetch=3,
                grid=(count,),
                in_specs=[whole, whole, panel_spec, panel_spec],
                out_specs=pl.BlockSpec(
                    (1, 2, CAP, BLK, BLK), lambda i, ds, tab, cr: (i, 0, 0, 0, 0)
                ),
            ),
            name="partial",
            cost_estimate=cost(count * 8 * 2 * BLK * BLK * 2 * rows, count << 18),
        )(dests, table, core_arr, hidden_t, hidden_other, panel, panel_other)

    def added(part, running):
        return (part.astype(jnp.float32) + running.astype(jnp.float32)).astype(jnp.bfloat16)

    half = ring_y // 2
    send_up = partials(half)[0]
    down = None
    for d in range(half, 0, -1):
        up = y_step(send_up, 1)
        if d == half:
            part = partials(d - 1, 1 - d)
            send_down = part[1]
            send_up = added(part[0], up)
            continue
        down = y_step(send_down, -1)
        if d > 1:
            part = partials(d - 1, 1 - d)
            send_up = added(part[0], up)
            send_down = added(part[1], down)
    here = partials(0)
    own_sum, send_sum = pl.pallas_call(
        combine_kernel,
        out_shape=(shape((CAP, BLK, BLK), jnp.float32), shape((CAP, BLK, BLK))),
        in_specs=[SMEM, VMEM, VMEM, VMEM],
        out_specs=(VMEM, VMEM),
        name="combine",
        cost_estimate=cost(1000, 1 << 20),
    )(xh.reshape(1).astype(jnp.int32), here, up, down)
    other_sum = swap_xh(send_sum)

    groups = 4
    per_group = shard_count // groups
    acc_spec = pl.BlockSpec((rows, units), lambda i, tab, cr: (0, 0))
    panel_spec = pl.BlockSpec((rows, width // groups), lambda i, tab, cr: (0, i))
    own_part, sent_part = pl.pallas_call(
        hidden_grad_kernel,
        out_shape=(shape((rows, units), jnp.float32), shape((rows, units), jnp.float32)),
        grid_spec=pltpu.PrefetchScalarGridSpec(
            num_scalar_prefetch=2,
            grid=(groups,),
            in_specs=[
                panel_spec,
                panel_spec,
                pl.BlockSpec((per_group, CAP, BLK, BLK), lambda i, tab, cr: (i, 0, 0, 0)),
            ],
            out_specs=(acc_spec, acc_spec),
        ),
        name="hidden_grad",
        cost_estimate=cost(shard_count * CAP * 4 * rows * BLK * BLK, 6 << 20),
    )(table, core_arr, panel, panel_other, weights)
    other_part = swap_core(sent_part)
    d_gate, d_up = pl.pallas_call(
        gates_kernel,
        out_shape=(shape((rows, units)), shape((rows, units))),
        in_specs=[VMEM] * 4,
        out_specs=(VMEM, VMEM),
        name="gates",
        cost_estimate=cost(1000, 3 << 19),
    )(own_part, other_part, gate_pre, up_pre)
    d_weight = pl.pallas_call(
        place_kernel,
        out_shape=shape(down_weight.shape),
        in_specs=[SMEM, SMEM, VMEM, VMEM],
        out_specs=VMEM,
        name="place",
        cost_estimate=cost(1000, 1 << 20),
    )(f_arr, tile_mask, own_sum, other_sum)
    return (d_gate, d_up, d_weight)


def solution(mesh):
    return jax.shard_map(
        per_device,
        mesh=mesh,
        in_specs=(
            P(("fsdp", "tensor"), None),
            P(("fsdp", "tensor")),
            P("fsdp", "tensor"),
            P("fsdp", "tensor"),
            P("tensor", "fsdp"),
            P("tensor", None),
        ),
        out_specs=(P("fsdp", "tensor"), P("fsdp", "tensor"), P("tensor", "fsdp")),
        check_vma=False,
    )
```

```python
import math

import jax
import jax.numpy as jnp
from jax import lax
from jax.experimental import pallas as pl
from jax.experimental.pallas import tpu as pltpu
from jax.sharding import PartitionSpec as P


BLK = 128
CAP = 4
TAB = 8


VMEM = pl.BlockSpec(memory_space=pltpu.VMEM)
SMEM = pl.BlockSpec(memory_space=pltpu.SMEM)


def prep_kernel(f_ref, live_ref, mask_ref, grad_ref, weight_ref, masked_ref, packed_ref):
    row_blocks = mask_ref.shape[0]
    rows = lax.broadcasted_iota(jnp.int32, grad_ref.shape, 0)
    value = grad_ref[...].astype(jnp.float32)
    masked_ref[...] = jnp.where(rows < live_ref[0], value, 0.0).astype(jnp.bfloat16)
    packed_ref[...] = jnp.zeros_like(packed_ref)
    count = jnp.int32(0)
    for r in range(row_blocks):
        for c in range(2):
            kept = mask_ref[r, 2 * f_ref[0] + c]

            @pl.when(kept == 1)
            def _(r=r, c=c, count=count):
                packed_ref[count] = weight_ref[
                    r * BLK : (r + 1) * BLK, c * BLK : (c + 1) * BLK
                ]

            count = count + kept


def table_kernel(f_ref, mask_ref, gate_ref, up_ref, table_ref, hidden_ref):
    row_blocks = mask_ref.shape[0]
    core = lax.rem(f_ref[0], 2)

    def one_shard(s, carry):
        f = 2 * s + core
        base = s * TAB
        for k in range(TAB):
            table_ref[base + k] = 0
        count = jnp.int32(0)
        for r in range(row_blocks):
            for c in range(2):
                table_ref[base + count] = 2 * r + c
                count = count + mask_ref[r, 2 * f + c]
        return carry

    lax.fori_loop(0, table_ref.shape[0] // TAB, one_shard, 0)
    gate = gate_ref[...].astype(jnp.float32)
    up = up_ref[...].astype(jnp.float32)
    hidden = gate * jax.nn.sigmoid(gate) * up
    hidden_ref[...] = hidden.T.astype(jnp.bfloat16)


def partial_kernel(scale, table_ref, core_ref, own_h, other_h, own_p, other_p, out_ref):
    dest = pl.program_id(0)
    wide = 2 * BLK
    for xh in range(2):
        s = 2 * dest + xh
        at = pl.multiple_of((2 * xh + core_ref[0]) * wide, wide)
        right = jnp.concatenate([own_p[:, pl.ds(at, wide)], other_p[:, pl.ds(at, wide)]], axis=0)
        places = [table_ref[s * TAB + k] for k in range(CAP)]
        rows = [pl.multiple_of((b >> 1) * BLK, BLK) for b in places]
        left = jnp.concatenate(
            [
                jnp.concatenate([own_h[pl.ds(r, BLK), :], other_h[pl.ds(r, BLK), :]], axis=1)
                for r in rows
            ],
            axis=0,
        )
        term = jnp.dot(left, right, preferred_element_type=jnp.float32) * scale
        for k, b in enumerate(places):
            tile = term[k * BLK : (k + 1) * BLK]
            kept = jnp.where((b & 1) == 0, tile[:, :BLK], tile[:, BLK:])
            out_ref[0, xh, k] = kept.astype(jnp.bfloat16)


def hidden_grad_kernel(
    table_ref, core_ref, own_p, other_p, weight_ref, own_ref, other_ref
):
    group = pl.program_id(0)
    shards = weight_ref.shape[0]
    wide = 2 * BLK
    rows = own_p.shape[0]

    @pl.when(group == 0)
    def _():
        own_ref[...] = jnp.zeros_like(own_ref)
        other_ref[...] = jnp.zeros_like(other_ref)

    for i in range(shards):
        s = group * shards + i
        at = pl.multiple_of((2 * i + core_ref[0]) * wide, wide)
        left = jnp.concatenate([own_p[:, pl.ds(at, wide)], other_p[:, pl.ds(at, wide)]], axis=0)
        places = [table_ref[s * TAB + k] for k in range(CAP)]
        halves = []
        for k, b in enumerate(places):
            tile = weight_ref[i, k].astype(jnp.float32)
            second = (b & 1) == 1
            zero = jnp.zeros_like(tile)
            halves.append(
                jnp.concatenate(
                    [jnp.where(second, zero, tile), jnp.where(second, tile, zero)], axis=1
                ).astype(jnp.bfloat16)
            )
        term = lax.dot_general(
            left,
            jnp.concatenate(halves, axis=0),
            (((1,), (1,)), ((), ())),
            preferred_element_type=jnp.float32,
        )
        for k, b in enumerate(places):
            r = pl.multiple_of((b >> 1) * BLK, BLK)
            part = term[:, k * BLK : (k + 1) * BLK]
            own_ref[:, pl.ds(r, BLK)] += part[:rows]
            other_ref[:, pl.ds(r, BLK)] += part[rows:]


def gates_kernel(own_ref, other_ref, gate_ref, up_ref, d_gate_ref, d_up_ref):
    d_hidden = own_ref[...] + other_ref[...]
    gate = gate_ref[...].astype(jnp.float32)
    up = up_ref[...].astype(jnp.float32)
    s = jax.nn.sigmoid(gate)
    d_up_ref[...] = (d_hidden * gate * s).astype(jnp.bfloat16)
    d_gate_ref[...] = (d_hidden * up * s * (1.0 + gate * (1.0 - s))).astype(jnp.bfloat16)


def place_kernel(f_ref, mask_ref, own_ref, other_ref, out_ref):
    row_blocks = mask_ref.shape[0]
    xh = (f_ref[0] >> 1) & 1
    out_ref[...] = jnp.zeros_like(out_ref)
    count = jnp.int32(0)
    for r in range(row_blocks):
        for c in range(2):
            kept = mask_ref[r, 2 * f_ref[0] + c]

            @pl.when(kept == 1)
            def _(r=r, c=c, count=count):
                total = own_ref[xh, count].astype(jnp.float32) + other_ref[count].astype(
                    jnp.float32
                )
                out_ref[r * BLK : (r + 1) * BLK, c * BLK : (c + 1) * BLK] = total.astype(
                    jnp.bfloat16
                )

            count = count + kept


def shape(dims, dtype=jnp.bfloat16):
    return jax.ShapeDtypeStruct(dims, dtype)


def cost(flops, size):
    return pl.CostEstimate(flops=flops, bytes_accessed=size, transcendentals=0)


def per_device(out_grad, live_rows, gate_pre, up_pre, down_weight, tile_mask):
    fsdp_count = lax.axis_size("fsdp")
    tensor_count = lax.axis_size("tensor")
    f = lax.axis_index("fsdp")
    t = lax.axis_index("tensor")
    ring_y = fsdp_count // 4
    ring_z = tensor_count // 2
    xh = (f >> 1) & 1
    xl, z = t >> (ring_z.bit_length() - 1), t & (ring_z - 1)
    tok, width = out_grad.shape
    rows, units = gate_pre.shape
    scale = 1.0 / math.sqrt(rows * fsdp_count)
    f_arr = f.reshape(1).astype(jnp.int32)

    def over_f(x, move):
        return lax.ppermute(x, "fsdp", [(i, move(i)) for i in range(fsdp_count)])

    def over_t(x, move):
        return lax.ppermute(x, "tensor", [(i, move(i)) for i in range(tensor_count)])

    def z_step(x, d):
        return over_t(x, lambda i: (i // ring_z) * ring_z + (i + d) % ring_z)

    def swap_core(x):
        return over_f(x, lambda i: i ^ 1)

    def swap_xh(x):
        return over_f(x, lambda i: i ^ 2)

    def swap_xl(x):
        return over_t(x, lambda i: (i + ring_z) % tensor_count)

    masked, packed = pl.pallas_call(
        prep_kernel,
        out_shape=(shape((tok, width)), shape((CAP, BLK, BLK))),
        in_specs=[SMEM, SMEM, SMEM, VMEM, VMEM],
        out_specs=(VMEM, VMEM),
        name="prep",
        cost_estimate=cost(1000, 1 << 20),
    )(f_arr, live_rows, tile_mask, out_grad, down_weight)
    masked_other = swap_xl(masked)
    packed_other = swap_xh(packed)

    shard_count = fsdp_count // 2
    table, hidden_t = pl.pallas_call(
        table_kernel,
        out_shape=(shape((shard_count * TAB,), jnp.int32), shape((units, rows))),
        in_specs=[SMEM, SMEM, VMEM, VMEM],
        out_specs=(SMEM, VMEM),
        name="hidden",
        cost_estimate=cost(1000, 1 << 20),
    )(f_arr, tile_mask, gate_pre, up_pre)
    hidden_other = swap_core(hidden_t)

    def pair(own, other, index):
        first = jnp.where(index == 0, own, other)
        second = jnp.where(index == 0, other, own)
        return jnp.stack([first, second])

    def gather(block, step, index, count):
        full = jnp.zeros((2, count) + block.shape[1:], block.dtype)

        def put(full, piece, at):
            start = (0, at & (count - 1)) + (0,) * (block.ndim - 1)
            return lax.dynamic_update_slice(full, piece[:, None], start)

        full = put(full, block, index)
        up = down = block
        for d in range(1, count // 2 + 1):
            up = step(up, 1)
            full = put(full, up, index - d + count)
            if d < count // 2:
                down = step(down, -1)
                full = put(full, down, index + d)
        return full

    panel = gather(pair(masked, masked_other, xl), z_step, z, ring_z).reshape(rows, width)
    columns = [[k + 4 * i for i in range(ring_y)] for k in range(4)]
    weights = lax.all_gather(
        pair(packed, packed_other, xh), "fsdp", axis_index_groups=columns, tiled=True
    )
    panel_other = swap_core(panel)
    core_arr = (f & 1).reshape(1).astype(jnp.int32)

    panel_spec = pl.BlockSpec((rows, width // ring_y), lambda i, tab, cr: (0, i))
    whole = pl.BlockSpec((units, rows), lambda i, tab, cr: (0, 0))

    def body(*refs):
        partial_kernel(scale, *refs)

    tiles = pl.pallas_call(
        body,
        out_shape=shape((ring_y, 2, CAP, BLK, BLK)),
        grid_spec=pltpu.PrefetchScalarGridSpec(
            num_scalar_prefetch=2,
            grid=(ring_y,),
            in_specs=[whole, whole, panel_spec, panel_spec],
            out_specs=pl.BlockSpec(
                (1, 2, CAP, BLK, BLK), lambda i, tab, cr: (i, 0, 0, 0, 0)
            ),
        ),
        name="partial",
        cost_estimate=cost(ring_y * 16 * BLK * BLK * 2 * rows, ring_y << 19),
    )(table, core_arr, hidden_t, hidden_other, panel, panel_other)
    sums = lax.psum_scatter(
        tiles, "fsdp", scatter_dimension=0, axis_index_groups=columns, tiled=True
    )[0]
    send_sum = lax.dynamic_index_in_dim(sums, 1 - xh, 0, keepdims=False)
    other_sum = swap_xh(send_sum)

    groups = 4
    per_group = shard_count // groups
    acc_spec = pl.BlockSpec((rows, units), lambda i, tab, cr: (0, 0))
    panel_spec = pl.BlockSpec((rows, width // groups), lambda i, tab, cr: (0, i))
    own_part, sent_part = pl.pallas_call(
        hidden_grad_kernel,
        out_shape=(shape((rows, units), jnp.float32), shape((rows, units), jnp.float32)),
        grid_spec=pltpu.PrefetchScalarGridSpec(
            num_scalar_prefetch=2,
            grid=(groups,),
            in_specs=[
                panel_spec,
                panel_spec,
                pl.BlockSpec((per_group, CAP, BLK, BLK), lambda i, tab, cr: (i, 0, 0, 0)),
            ],
            out_specs=(acc_spec, acc_spec),
        ),
        name="hidden_grad",
        cost_estimate=cost(shard_count * CAP * 4 * rows * BLK * BLK, 6 << 20),
    )(table, core_arr, panel, panel_other, weights)
    other_part = swap_core(sent_part)
    d_gate, d_up = pl.pallas_call(
        gates_kernel,
        out_shape=(shape((rows, units)), shape((rows, units))),
        in_specs=[VMEM] * 4,
        out_specs=(VMEM, VMEM),
        name="gates",
        cost_estimate=cost(1000, 3 << 19),
    )(own_part, other_part, gate_pre, up_pre)
    d_weight = pl.pallas_call(
        place_kernel,
        out_shape=shape(down_weight.shape),
        in_specs=[SMEM, SMEM, VMEM, VMEM],
        out_specs=VMEM,
        name="place",
        cost_estimate=cost(1000, 1 << 20),
    )(f_arr, tile_mask, sums, other_sum)
    return (d_gate, d_up, d_weight)


def solution(mesh):
    return jax.shard_map(
        per_device,
        mesh=mesh,
        in_specs=(
            P(("fsdp", "tensor"), None),
            P(("fsdp", "tensor")),
            P("fsdp", "tensor"),
            P("fsdp", "tensor"),
            P("tensor", "fsdp"),
            P("tensor", None),
        ),
        out_specs=(P("fsdp", "tensor"), P("fsdp", "tensor"), P("tensor", "fsdp")),
        check_vma=False,
    )
```

```python
import functools
import math

import jax
import jax.numpy as jnp
from jax import lax
from jax.experimental import pallas as pl
from jax.experimental.pallas import tpu as pltpu
from jax.sharding import PartitionSpec as P


BLK = 128
CAP = 4
TAB = 8
TOK = 8


VMEM = pl.BlockSpec(memory_space=pltpu.VMEM)
SMEM = pl.BlockSpec(memory_space=pltpu.SMEM)


def by_ring(x):
    rows, width = x.shape
    return jnp.swapaxes(x.reshape(2, rows // (2 * TOK), TOK, width), 0, 1).reshape(rows, width)


def by_token(x):
    rows, width = x.shape
    return jnp.swapaxes(x.reshape(rows // (2 * TOK), 2, TOK, width), 0, 1).reshape(rows, width)


def prep_kernel(f_ref, live_ref, mask_ref, grad_ref, weight_ref, masked_ref, packed_ref):
    row_blocks = mask_ref.shape[0]
    rows = lax.broadcasted_iota(jnp.int32, grad_ref.shape, 0)
    value = grad_ref[...].astype(jnp.float32)
    masked_ref[...] = jnp.where(rows < live_ref[0], value, 0.0).astype(jnp.bfloat16)
    packed_ref[...] = jnp.zeros_like(packed_ref)
    count = jnp.int32(0)
    for r in range(row_blocks):
        for c in range(2):
            kept = mask_ref[r, 2 * f_ref[0] + c]

            @pl.when(kept == 1)
            def _(r=r, c=c, count=count):
                packed_ref[count] = weight_ref[
                    r * BLK : (r + 1) * BLK, c * BLK : (c + 1) * BLK
                ]

            count = count + kept


def table_kernel(f_ref, mask_ref, gate_ref, up_ref, table_ref, hidden_ref):
    row_blocks = mask_ref.shape[0]
    core = lax.rem(f_ref[0], 2)

    def one_shard(s, carry):
        f = 2 * s + core
        base = s * TAB
        for k in range(TAB):
            table_ref[base + k] = 0
        count = jnp.int32(0)
        for r in range(row_blocks):
            for c in range(2):
                table_ref[base + count] = 2 * r + c
                count = count + mask_ref[r, 2 * f + c]
        return carry

    lax.fori_loop(0, table_ref.shape[0] // TAB, one_shard, 0)
    gate = gate_ref[...].astype(jnp.float32)
    up = up_ref[...].astype(jnp.float32)
    hidden = gate * jax.nn.sigmoid(gate) * up
    hidden_ref[...] = by_ring(hidden).T.astype(jnp.bfloat16)


def partial_kernel(table_ref, core_ref, hidden_ref, panel_ref, out_ref):
    dest = pl.program_id(0)
    wide = 2 * BLK
    for xh in range(2):
        s = 2 * dest + xh
        at = pl.multiple_of((2 * xh + core_ref[0]) * wide, wide)
        right = panel_ref[:, pl.ds(at, wide)]
        places = [table_ref[s * TAB + k] for k in range(CAP)]
        rows = [pl.multiple_of((b >> 1) * BLK, BLK) for b in places]
        left = jnp.concatenate(
            [
                jnp.concatenate([hidden_ref[c, pl.ds(r, BLK), :] for c in range(2)], axis=1)
                for r in rows
            ],
            axis=0,
        )
        term = jnp.dot(left, right, preferred_element_type=jnp.float32)
        for k, b in enumerate(places):
            tile = term[k * BLK : (k + 1) * BLK]
            kept = jnp.where((b & 1) == 0, tile[:, :BLK], tile[:, BLK:])
            out_ref[0, xh, k] = kept.astype(jnp.bfloat16)


def hidden_grad_kernel(
    table_ref, core_ref, panel_ref, weight_ref, own_ref, other_ref, sum_ref
):
    group = pl.program_id(0)
    shards = weight_ref.shape[0]
    wide = 2 * BLK
    rows = own_ref.shape[0]

    @pl.when(group == 0)
    def _():
        sum_ref[...] = jnp.zeros_like(sum_ref)

    for i in range(shards):
        s = group * shards + i
        at = pl.multiple_of((2 * i + core_ref[0]) * wide, wide)
        left = panel_ref[:, pl.ds(at, wide)]
        places = [table_ref[s * TAB + k] for k in range(CAP)]
        halves = []
        for k, b in enumerate(places):
            tile = weight_ref[i, k].astype(jnp.float32)
            second = (b & 1) == 1
            zero = jnp.zeros_like(tile)
            halves.append(
                jnp.concatenate(
                    [jnp.where(second, zero, tile), jnp.where(second, tile, zero)], axis=1
                ).astype(jnp.bfloat16)
            )
        term = lax.dot_general(
            left,
            jnp.concatenate(halves, axis=0),
            (((1,), (1,)), ((), ())),
            preferred_element_type=jnp.float32,
        )
        for k, b in enumerate(places):
            r = pl.multiple_of((b >> 1) * BLK, BLK)
            part = term[:, k * BLK : (k + 1) * BLK]
            sum_ref[0, :, pl.ds(r, BLK)] += part[:rows]
            sum_ref[1, :, pl.ds(r, BLK)] += part[rows:]

    @pl.when(group == pl.num_programs(0) - 1)
    def _():
        own_ref[...] = sum_ref[core_ref[0]]
        other_ref[...] = sum_ref[1 - core_ref[0]]


def gates_kernel(own_ref, other_ref, gate_ref, up_ref, d_gate_ref, d_up_ref):
    d_hidden = by_token(own_ref[...] + other_ref[...])
    gate = gate_ref[...].astype(jnp.float32)
    up = up_ref[...].astype(jnp.float32)
    s = jax.nn.sigmoid(gate)
    d_up_ref[...] = (d_hidden * gate * s).astype(jnp.bfloat16)
    d_gate_ref[...] = (d_hidden * up * s * (1.0 + gate * (1.0 - s))).astype(jnp.bfloat16)


def place_kernel(scale, f_ref, mask_ref, own_ref, other_ref, out_ref):
    row_blocks = mask_ref.shape[0]
    xh = (f_ref[0] >> 1) & 1
    out_ref[...] = jnp.zeros_like(out_ref)
    count = jnp.int32(0)
    for r in range(row_blocks):
        for c in range(2):
            kept = mask_ref[r, 2 * f_ref[0] + c]

            @pl.when(kept == 1)
            def _(r=r, c=c, count=count):
                total = own_ref[xh, count].astype(jnp.float32) + other_ref[count].astype(
                    jnp.float32
                )
                out_ref[r * BLK : (r + 1) * BLK, c * BLK : (c + 1) * BLK] = (
                    total * scale
                ).astype(jnp.bfloat16)

            count = count + kept


def shape(dims, dtype=jnp.bfloat16):
    return jax.ShapeDtypeStruct(dims, dtype)


def cost(flops, size):
    return pl.CostEstimate(flops=flops, bytes_accessed=size, transcendentals=0)


def per_device(out_grad, live_rows, gate_pre, up_pre, down_weight, tile_mask):
    fsdp_count = lax.axis_size("fsdp")
    tensor_count = lax.axis_size("tensor")
    f = lax.axis_index("fsdp")
    t = lax.axis_index("tensor")
    ring_y = fsdp_count // 4
    ring_z = tensor_count // 2
    y, xh = f >> 2, (f >> 1) & 1
    xl = t >> (ring_z.bit_length() - 1)
    tok, width = out_grad.shape
    rows, units = gate_pre.shape
    scale = 1.0 / math.sqrt(rows * fsdp_count)
    f_arr = f.reshape(1).astype(jnp.int32)

    def over_f(x, move):
        return lax.ppermute(x, "fsdp", [(i, move(i)) for i in range(fsdp_count)])

    def over_t(x, move):
        return lax.ppermute(x, "tensor", [(i, move(i)) for i in range(tensor_count)])

    def y_step(x, d):
        return over_f(x, lambda i: (i + 4 * d) % fsdp_count)

    def swap_core(x):
        return over_f(x, lambda i: i ^ 1)

    def swap_xh(x):
        return over_f(x, lambda i: i ^ 2)

    def swap_xl(x):
        return over_t(x, lambda i: (i + ring_z) % tensor_count)

    masked, packed = pl.pallas_call(
        prep_kernel,
        out_shape=(shape((tok, width)), shape((CAP, BLK, BLK))),
        in_specs=[SMEM, SMEM, SMEM, VMEM, VMEM],
        out_specs=(VMEM, VMEM),
        name="prep",
        cost_estimate=cost(1000, 1 << 20),
    )(f_arr, live_rows, tile_mask, out_grad, down_weight)
    masked_other = swap_xl(masked)
    packed_other = swap_xh(packed)

    shard_count = fsdp_count // 2
    table, hidden_t = pl.pallas_call(
        table_kernel,
        out_shape=(shape((shard_count * TAB,), jnp.int32), shape((units, rows))),
        in_specs=[SMEM, SMEM, VMEM, VMEM],
        out_specs=(SMEM, VMEM),
        name="hidden",
        cost_estimate=cost(1000, 1 << 20),
    )(f_arr, tile_mask, gate_pre, up_pre)
    hidden_other = swap_core(hidden_t)

    def pair(own, other, index):
        first = jnp.where(index == 0, own, other)
        second = jnp.where(index == 0, other, own)
        return jnp.stack([first, second])

    columns = [[k + 4 * i for i in range(ring_y)] for k in range(4)]
    chips = [
        [(2 * i + c) * tensor_count + half * ring_z + j for c in range(2) for j in range(ring_z)]
        for i in range(fsdp_count // 2)
        for half in range(2)
    ]
    panel = lax.all_gather(
        pair(masked, masked_other, xl),
        ("fsdp", "tensor"),
        axis_index_groups=chips,
        tiled=True,
    ).reshape(2 * rows, width)
    hidden_pair = pair(hidden_t, hidden_other, f & 1)

    weights = jnp.zeros((ring_y, 2, CAP, BLK, BLK), jnp.bfloat16)

    def put(full, piece, at):
        return lax.dynamic_update_slice(full, piece[None], (at & (ring_y - 1), 0, 0, 0, 0))

    up = down = pair(packed, packed_other, xh)
    weights = put(weights, up, y)
    for d in range(1, ring_y // 2 + 1):
        up = y_step(up, 1)
        weights = put(weights, up, y - d + ring_y)
        if d < ring_y // 2:
            down = y_step(down, -1)
            weights = put(weights, down, y + d)
    weights = weights.reshape(shard_count, CAP, BLK, BLK)
    core_arr = (f & 1).reshape(1).astype(jnp.int32)

    panel_spec = pl.BlockSpec((2 * rows, width // ring_y), lambda i, tab, cr: (0, i))
    whole = pl.BlockSpec((2, units, rows), lambda i, tab, cr: (0, 0, 0))
    tiles = pl.pallas_call(
        partial_kernel,
        out_shape=shape((ring_y, 2, CAP, BLK, BLK)),
        grid_spec=pltpu.PrefetchScalarGridSpec(
            num_scalar_prefetch=2,
            grid=(ring_y,),
            in_specs=[whole, panel_spec],
            out_specs=pl.BlockSpec(
                (1, 2, CAP, BLK, BLK), lambda i, tab, cr: (i, 0, 0, 0, 0)
            ),
        ),
        name="partial",
        cost_estimate=cost(ring_y * 16 * BLK * BLK * 2 * rows, ring_y << 19),
    )(table, core_arr, hidden_pair, panel)
    sums = lax.psum_scatter(
        tiles, "fsdp", scatter_dimension=0, axis_index_groups=columns, tiled=True
    )[0]
    send_sum = lax.dynamic_index_in_dim(sums, 1 - xh, 0, keepdims=False)
    other_sum = swap_xh(send_sum)

    groups = 4
    per_group = shard_count // groups
    acc_spec = pl.BlockSpec((rows, units), lambda i, tab, cr: (0, 0))
    panel_spec = pl.BlockSpec((2 * rows, width // groups), lambda i, tab, cr: (0, i))
    own_part, sent_part = pl.pallas_call(
        hidden_grad_kernel,
        out_shape=(shape((rows, units), jnp.float32), shape((rows, units), jnp.float32)),
        grid_spec=pltpu.PrefetchScalarGridSpec(
            num_scalar_prefetch=2,
            grid=(groups,),
            in_specs=[
                panel_spec,
                pl.BlockSpec((per_group, CAP, BLK, BLK), lambda i, tab, cr: (i, 0, 0, 0)),
            ],
            out_specs=(acc_spec, acc_spec),
            scratch_shapes=[pltpu.VMEM((2, rows, units), jnp.float32)],
        ),
        name="hidden_grad",
        cost_estimate=cost(shard_count * CAP * 4 * rows * BLK * BLK, 6 << 20),
    )(table, core_arr, panel, weights)
    other_part = swap_core(sent_part)
    d_gate, d_up = pl.pallas_call(
        gates_kernel,
        out_shape=(shape((rows, units)), shape((rows, units))),
        in_specs=[VMEM] * 4,
        out_specs=(VMEM, VMEM),
        name="gates",
        cost_estimate=cost(1000, 3 << 19),
    )(own_part, other_part, gate_pre, up_pre)
    d_weight = pl.pallas_call(
        functools.partial(place_kernel, scale),
        out_shape=shape(down_weight.shape),
        in_specs=[SMEM, SMEM, VMEM, VMEM],
        out_specs=VMEM,
        name="place",
        cost_estimate=cost(1000, 1 << 20),
    )(f_arr, tile_mask, sums, other_sum)
    return (d_gate, d_up, d_weight)


def solution(mesh):
    return jax.shard_map(
        per_device,
        mesh=mesh,
        in_specs=(
            P(("fsdp", "tensor"), None),
            P(("fsdp", "tensor")),
            P("fsdp", "tensor"),
            P("fsdp", "tensor"),
            P("tensor", "fsdp"),
            P("tensor", None),
        ),
        out_specs=(P("fsdp", "tensor"), P("fsdp", "tensor"), P("tensor", "fsdp")),
        check_vma=False,
    )
```

```python
import functools
import math

import jax
import jax.numpy as jnp
from jax import lax
from jax.experimental import pallas as pl
from jax.experimental.pallas import tpu as pltpu
from jax.sharding import PartitionSpec as P


BLK = 128
CAP = 4
TAB = 8
TOK = 8


VMEM = pl.BlockSpec(memory_space=pltpu.VMEM)
SMEM = pl.BlockSpec(memory_space=pltpu.SMEM)


def by_ring(x):
    rows, width = x.shape
    return jnp.swapaxes(x.reshape(2, rows // (2 * TOK), TOK, width), 0, 1).reshape(rows, width)


def by_token(x):
    rows, width = x.shape
    return jnp.swapaxes(x.reshape(rows // (2 * TOK), 2, TOK, width), 0, 1).reshape(rows, width)


def pack_kernel(f_ref, mask_ref, weight_ref, packed_ref):
    row_blocks = mask_ref.shape[0]
    packed_ref[...] = jnp.zeros_like(packed_ref)
    count = jnp.int32(0)
    for r in range(row_blocks):
        for c in range(2):
            kept = mask_ref[r, 2 * f_ref[0] + c]

            @pl.when(kept == 1)
            def _(r=r, c=c, count=count):
                packed_ref[count] = weight_ref[
                    r * BLK : (r + 1) * BLK, c * BLK : (c + 1) * BLK
                ]

            count = count + kept


def table_kernel(f_ref, mask_ref, gate_ref, up_ref, table_ref, hidden_ref):
    row_blocks = mask_ref.shape[0]
    core = lax.rem(f_ref[0], 2)

    def one_shard(s, carry):
        f = 2 * s + core
        base = s * TAB
        for k in range(TAB):
            table_ref[base + k] = 0
        count = jnp.int32(0)
        for r in range(row_blocks):
            for c in range(2):
                table_ref[base + count] = 2 * r + c
                count = count + mask_ref[r, 2 * f + c]
        return carry

    lax.fori_loop(0, table_ref.shape[0] // TAB, one_shard, 0)
    gate = gate_ref[...].astype(jnp.float32)
    up = up_ref[...].astype(jnp.float32)
    hidden = gate * jax.nn.sigmoid(gate) * up
    hidden_ref[...] = by_ring(hidden).T.astype(jnp.bfloat16)


def partial_kernel(table_ref, core_ref, hidden_ref, panel_ref, out_ref):
    count = out_ref.shape[0]
    wide = 2 * BLK
    for i in range(count):
        dest = pl.program_id(0) * count + i
        for flip in range(2):
            xh = flip ^ core_ref[1]
            s = 2 * dest + xh
            at = pl.multiple_of(i * 4 * wide + (2 * xh + core_ref[0]) * wide, wide)
            right = panel_ref[:, pl.ds(at, wide)]
            places = [table_ref[s * TAB + k] for k in range(CAP)]
            rows = [pl.multiple_of((b >> 1) * BLK, BLK) for b in places]
            left = jnp.concatenate(
                [
                    jnp.concatenate([hidden_ref[c, pl.ds(r, BLK), :] for c in range(2)], axis=1)
                    for r in rows
                ],
                axis=0,
            )
            term = jnp.dot(left, right, preferred_element_type=jnp.float32)
            for k, b in enumerate(places):
                tile = term[k * BLK : (k + 1) * BLK]
                kept = jnp.where((b & 1) == 0, tile[:, :BLK], tile[:, BLK:])
                out_ref[i, flip, k] = kept.astype(jnp.bfloat16)


def hidden_grad_kernel(
    table_ref, core_ref, panel_ref, weight_ref, own_ref, other_ref, sum_ref
):
    group = pl.program_id(0)
    shards = weight_ref.shape[0]
    wide = 2 * BLK
    rows = own_ref.shape[0]

    @pl.when(group == 0)
    def _():
        sum_ref[...] = jnp.zeros_like(sum_ref)

    for i in range(shards):
        s = group * shards + i
        at = pl.multiple_of((2 * i + core_ref[0]) * wide, wide)
        left = panel_ref[:, pl.ds(at, wide)]
        places = [table_ref[s * TAB + k] for k in range(CAP)]
        halves = []
        for k, b in enumerate(places):
            tile = weight_ref[i, k].astype(jnp.float32)
            second = (b & 1) == 1
            zero = jnp.zeros_like(tile)
            halves.append(
                jnp.concatenate(
                    [jnp.where(second, zero, tile), jnp.where(second, tile, zero)], axis=1
                ).astype(jnp.bfloat16)
            )
        term = lax.dot_general(
            left,
            jnp.concatenate(halves, axis=0),
            (((1,), (1,)), ((), ())),
            preferred_element_type=jnp.float32,
        )
        for k, b in enumerate(places):
            r = pl.multiple_of((b >> 1) * BLK, BLK)
            part = term[:, k * BLK : (k + 1) * BLK]
            sum_ref[0, :, pl.ds(r, BLK)] += part[:rows]
            sum_ref[1, :, pl.ds(r, BLK)] += part[rows:]

    @pl.when(group == pl.num_programs(0) - 1)
    def _():
        own_ref[...] = sum_ref[core_ref[0]]
        other_ref[...] = sum_ref[1 - core_ref[0]]


def gates_kernel(own_ref, other_ref, gate_ref, up_ref, d_gate_ref, d_up_ref):
    d_hidden = by_token(own_ref[...] + other_ref[...])
    gate = gate_ref[...].astype(jnp.float32)
    up = up_ref[...].astype(jnp.float32)
    s = jax.nn.sigmoid(gate)
    d_up_ref[...] = (d_hidden * gate * s).astype(jnp.bfloat16)
    d_gate_ref[...] = (d_hidden * up * s * (1.0 + gate * (1.0 - s))).astype(jnp.bfloat16)


def place_kernel(scale, f_ref, mask_ref, own_ref, other_ref, out_ref):
    row_blocks = mask_ref.shape[0]
    out_ref[...] = jnp.zeros_like(out_ref)
    count = jnp.int32(0)
    for r in range(row_blocks):
        for c in range(2):
            kept = mask_ref[r, 2 * f_ref[0] + c]

            @pl.when(kept == 1)
            def _(r=r, c=c, count=count):
                total = own_ref[0, count].astype(jnp.float32) + other_ref[count].astype(
                    jnp.float32
                )
                out_ref[r * BLK : (r + 1) * BLK, c * BLK : (c + 1) * BLK] = (
                    total * scale
                ).astype(jnp.bfloat16)

            count = count + kept


def shape(dims, dtype=jnp.bfloat16):
    return jax.ShapeDtypeStruct(dims, dtype)


def cost(flops, size):
    return pl.CostEstimate(flops=flops, bytes_accessed=size, transcendentals=0)


def per_device(out_grad, live_rows, gate_pre, up_pre, down_weight, tile_mask):
    fsdp_count = lax.axis_size("fsdp")
    tensor_count = lax.axis_size("tensor")
    f = lax.axis_index("fsdp")
    t = lax.axis_index("tensor")
    ring_y = fsdp_count // 4
    ring_z = tensor_count // 2
    y, xh = f >> 2, (f >> 1) & 1
    xl = t >> (ring_z.bit_length() - 1)
    tok, width = out_grad.shape
    rows, units = gate_pre.shape
    scale = 1.0 / math.sqrt(rows * fsdp_count)
    f_arr = f.reshape(1).astype(jnp.int32)

    def over_f(x, move):
        return lax.ppermute(x, "fsdp", [(i, move(i)) for i in range(fsdp_count)])

    def over_t(x, move):
        return lax.ppermute(x, "tensor", [(i, move(i)) for i in range(tensor_count)])

    def y_step(x, d):
        return over_f(x, lambda i: (i + 4 * d) % fsdp_count)

    def swap_core(x):
        return over_f(x, lambda i: i ^ 1)

    def swap_xh(x):
        return over_f(x, lambda i: i ^ 2)

    def swap_xl(x):
        return over_t(x, lambda i: (i + ring_z) % tensor_count)

    grad_other = swap_xl(out_grad)
    live_other = swap_xl(live_rows)
    packed = pl.pallas_call(
        pack_kernel,
        out_shape=shape((CAP, BLK, BLK)),
        in_specs=[SMEM, SMEM, VMEM],
        out_specs=VMEM,
        name="pack",
        cost_estimate=cost(1000, 1 << 20),
    )(f_arr, tile_mask, down_weight)
    packed_other = swap_xh(packed)

    shard_count = fsdp_count // 2
    table, hidden_t = pl.pallas_call(
        table_kernel,
        out_shape=(shape((shard_count * TAB,), jnp.int32), shape((units, rows))),
        in_specs=[SMEM, SMEM, VMEM, VMEM],
        out_specs=(SMEM, VMEM),
        name="hidden",
        cost_estimate=cost(1000, 1 << 20),
    )(f_arr, tile_mask, gate_pre, up_pre)
    hidden_other = swap_core(hidden_t)

    def pair(own, other, index):
        first = (jnp.arange(2) == index).reshape((2,) + (1,) * own.ndim)
        return jnp.where(first, own[None], other[None])

    live = pair(live_rows, live_other, xl).reshape(2, 1, 1)
    masked = jnp.where(
        jnp.arange(tok)[None, :, None] < live,
        pair(out_grad, grad_other, xl),
        jnp.zeros((), jnp.bfloat16),
    )

    columns = [[k + 4 * i for i in range(ring_y)] for k in range(4)]
    chips = [
        [(2 * i + c) * tensor_count + half * ring_z + j for c in range(2) for j in range(ring_z)]
        for i in range(fsdp_count // 2)
        for half in range(2)
    ]
    panel = lax.all_gather(
        masked,
        ("fsdp", "tensor"),
        axis_index_groups=chips,
        tiled=True,
    ).reshape(2 * rows, width)
    hidden_pair = pair(hidden_t, hidden_other, f & 1)

    weights = jnp.zeros((ring_y, 2, CAP, BLK, BLK), jnp.bfloat16)

    def put(full, piece, at):
        return lax.dynamic_update_slice(full, piece[None], (at & (ring_y - 1), 0, 0, 0, 0))

    up = down = pair(packed, packed_other, xh)
    weights = put(weights, up, y)
    for d in range(1, ring_y // 2 + 1):
        up = y_step(up, 1)
        weights = put(weights, up, y - d + ring_y)
        if d < ring_y // 2:
            down = y_step(down, -1)
            weights = put(weights, down, y + d)
    weights = weights.reshape(shard_count, CAP, BLK, BLK)
    core_arr = jnp.stack([f & 1, xh]).astype(jnp.int32)
    per_step = ring_y // 2

    panel_spec = pl.BlockSpec((2 * rows, width // ring_y * per_step), lambda i, tab, cr: (0, i))
    whole = pl.BlockSpec((2, units, rows), lambda i, tab, cr: (0, 0, 0))
    tiles = pl.pallas_call(
        partial_kernel,
        out_shape=shape((ring_y, 2, CAP, BLK, BLK)),
        grid_spec=pltpu.PrefetchScalarGridSpec(
            num_scalar_prefetch=2,
            grid=(ring_y // per_step,),
            in_specs=[whole, panel_spec],
            out_specs=pl.BlockSpec(
                (per_step, 2, CAP, BLK, BLK), lambda i, tab, cr: (i, 0, 0, 0, 0)
            ),
        ),
        name="partial",
        cost_estimate=cost(ring_y * 16 * BLK * BLK * 2 * rows, ring_y << 19),
    )(table, core_arr, hidden_pair, panel)
    sums = lax.psum_scatter(
        tiles, "fsdp", scatter_dimension=0, axis_index_groups=columns, tiled=True
    )[0]
    send_sum = sums[1]
    other_sum = swap_xh(send_sum)

    groups = 4
    per_group = shard_count // groups
    acc_spec = pl.BlockSpec((rows, units), lambda i, tab, cr: (0, 0))
    panel_spec = pl.BlockSpec((2 * rows, width // groups), lambda i, tab, cr: (0, i))
    own_part, sent_part = pl.pallas_call(
        hidden_grad_kernel,
        out_shape=(shape((rows, units), jnp.float32), shape((rows, units), jnp.float32)),
        grid_spec=pltpu.PrefetchScalarGridSpec(
            num_scalar_prefetch=2,
            grid=(groups,),
            in_specs=[
                panel_spec,
                pl.BlockSpec((per_group, CAP, BLK, BLK), lambda i, tab, cr: (i, 0, 0, 0)),
            ],
            out_specs=(acc_spec, acc_spec),
            scratch_shapes=[pltpu.VMEM((2, rows, units), jnp.float32)],
        ),
        name="hidden_grad",
        cost_estimate=cost(shard_count * CAP * 4 * rows * BLK * BLK, 6 << 20),
    )(table, core_arr, panel, weights)
    other_part = swap_core(sent_part)
    d_gate, d_up = pl.pallas_call(
        gates_kernel,
        out_shape=(shape((rows, units)), shape((rows, units))),
        in_specs=[VMEM] * 4,
        out_specs=(VMEM, VMEM),
        name="gates",
        compiler_params=pltpu.CompilerParams(vmem_limit_bytes=16 << 20),
        cost_estimate=cost(1000, 3 << 19),
    )(own_part, other_part, gate_pre, up_pre)
    d_weight = pl.pallas_call(
        functools.partial(place_kernel, scale),
        out_shape=shape(down_weight.shape),
        in_specs=[SMEM, SMEM, VMEM, VMEM],
        out_specs=VMEM,
        name="place",
        compiler_params=pltpu.CompilerParams(vmem_limit_bytes=16 << 20),
        cost_estimate=cost(1000, 1 << 20),
    )(f_arr, tile_mask, sums, other_sum)
    return (d_gate, d_up, d_weight)


def solution(mesh):
    return jax.shard_map(
        per_device,
        mesh=mesh,
        in_specs=(
            P(("fsdp", "tensor"), None),
            P(("fsdp", "tensor")),
            P("fsdp", "tensor"),
            P("fsdp", "tensor"),
            P("tensor", "fsdp"),
            P("tensor", None),
        ),
        out_specs=(P("fsdp", "tensor"), P("fsdp", "tensor"), P("tensor", "fsdp")),
        check_vma=False,
    )
```

```python
import functools
import math

import jax
import jax.numpy as jnp
from jax import lax
from jax.experimental import pallas as pl
from jax.experimental.pallas import tpu as pltpu
from jax.sharding import PartitionSpec as P


BLK = 128
CAP = 4
TAB = 8
TOK = 8


VMEM = pl.BlockSpec(memory_space=pltpu.VMEM)
SMEM = pl.BlockSpec(memory_space=pltpu.SMEM)


def by_ring(x):
    rows, width = x.shape
    return jnp.swapaxes(x.reshape(2, rows // (2 * TOK), TOK, width), 0, 1).reshape(rows, width)


def by_token(x):
    rows, width = x.shape
    return jnp.swapaxes(x.reshape(rows // (2 * TOK), 2, TOK, width), 0, 1).reshape(rows, width)


def pack_kernel(f_ref, mask_ref, weight_ref, packed_ref):
    row_blocks = mask_ref.shape[0]
    packed_ref[...] = jnp.zeros_like(packed_ref)
    count = jnp.int32(0)
    for r in range(row_blocks):
        for c in range(2):
            kept = mask_ref[r, 2 * f_ref[0] + c]

            @pl.when(kept == 1)
            def _(r=r, c=c, count=count):
                packed_ref[count] = weight_ref[
                    r * BLK : (r + 1) * BLK, c * BLK : (c + 1) * BLK
                ]

            count = count + kept


def table_kernel(f_ref, mask_ref, gate_ref, up_ref, table_ref, hidden_ref):
    row_blocks = mask_ref.shape[0]
    core = lax.rem(f_ref[0], 2)

    def one_shard(s, carry):
        f = 2 * s + core
        base = s * TAB
        for k in range(TAB):
            table_ref[base + k] = 0
        count = jnp.int32(0)
        for r in range(row_blocks):
            for c in range(2):
                table_ref[base + count] = 2 * r + c
                count = count + mask_ref[r, 2 * f + c]
        return carry

    lax.fori_loop(0, table_ref.shape[0] // TAB, one_shard, 0)
    gate = gate_ref[...].astype(jnp.float32)
    up = up_ref[...].astype(jnp.float32)
    hidden = gate * jax.nn.sigmoid(gate) * up
    hidden_ref[...] = by_ring(hidden).astype(jnp.bfloat16)


def join_kernel(core_ref, own_ref, other_ref, out_ref):
    rows, _ = own_ref.shape
    first = core_ref[0] == 0
    pieces = []
    for at in range(0, rows, 2 * TOK):
        own = own_ref[at : at + 2 * TOK, :].astype(jnp.float32)
        other = other_ref[at : at + 2 * TOK, :].astype(jnp.float32)
        pieces += [jnp.where(first, own, other), jnp.where(first, other, own)]
    out_ref[...] = jnp.concatenate(pieces, axis=0).T.astype(jnp.bfloat16)


def partial_kernel(table_ref, core_ref, hidden_ref, panel_ref, out_ref):
    count = out_ref.shape[0]
    wide = 2 * BLK
    for i in range(count):
        dest = pl.program_id(0) * count + i
        for flip in range(2):
            xh = flip ^ core_ref[1]
            s = 2 * dest + xh
            at = pl.multiple_of(i * 4 * wide + (2 * xh + core_ref[0]) * wide, wide)
            right = panel_ref[:, pl.ds(at, wide)]
            places = [table_ref[s * TAB + k] for k in range(CAP)]
            rows = [pl.multiple_of((b >> 1) * BLK, BLK) for b in places]
            left = jnp.concatenate([hidden_ref[pl.ds(r, BLK), :] for r in rows], axis=0)
            term = jnp.dot(left, right, preferred_element_type=jnp.float32)
            for k, b in enumerate(places):
                tile = term[k * BLK : (k + 1) * BLK]
                kept = jnp.where((b & 1) == 0, tile[:, :BLK], tile[:, BLK:])
                out_ref[i, flip, k] = kept.astype(jnp.bfloat16)


def hidden_grad_kernel(
    table_ref, core_ref, panel_ref, weight_ref, own_ref, other_ref, sum_ref
):
    group = pl.program_id(0)
    shards = weight_ref.shape[0]
    wide = 2 * BLK
    rows = own_ref.shape[0]

    @pl.when(group == 0)
    def _():
        sum_ref[...] = jnp.zeros_like(sum_ref)

    for i in range(shards):
        s = group * shards + i
        at = pl.multiple_of((2 * i + core_ref[0]) * wide, wide)
        left = panel_ref[:, pl.ds(at, wide)]
        places = [table_ref[s * TAB + k] for k in range(CAP)]
        halves = []
        for k, b in enumerate(places):
            tile = weight_ref[i, k].astype(jnp.float32)
            second = (b & 1) == 1
            zero = jnp.zeros_like(tile)
            halves.append(
                jnp.concatenate(
                    [jnp.where(second, zero, tile), jnp.where(second, tile, zero)], axis=1
                ).astype(jnp.bfloat16)
            )
        term = lax.dot_general(
            left,
            jnp.concatenate(halves, axis=0),
            (((1,), (1,)), ((), ())),
            preferred_element_type=jnp.float32,
        )
        for k, b in enumerate(places):
            r = pl.multiple_of((b >> 1) * BLK, BLK)
            part = term[:, k * BLK : (k + 1) * BLK]
            sum_ref[:, pl.ds(r, BLK)] += part

    @pl.when(group == pl.num_programs(0) - 1)
    def _():
        first = core_ref[0] == 0
        for at in range(0, rows, 2 * TOK):
            a = sum_ref[2 * at : 2 * at + 2 * TOK, :]
            b = sum_ref[2 * at + 2 * TOK : 2 * at + 4 * TOK, :]
            own_ref[at : at + 2 * TOK, :] = jnp.where(first, a, b)
            other_ref[at : at + 2 * TOK, :] = jnp.where(first, b, a)


def gates_kernel(own_ref, other_ref, gate_ref, up_ref, d_gate_ref, d_up_ref):
    d_hidden = by_token(own_ref[...] + other_ref[...])
    gate = gate_ref[...].astype(jnp.float32)
    up = up_ref[...].astype(jnp.float32)
    s = jax.nn.sigmoid(gate)
    d_up_ref[...] = (d_hidden * gate * s).astype(jnp.bfloat16)
    d_gate_ref[...] = (d_hidden * up * s * (1.0 + gate * (1.0 - s))).astype(jnp.bfloat16)


def place_kernel(scale, f_ref, mask_ref, own_ref, other_ref, out_ref):
    row_blocks = mask_ref.shape[0]
    out_ref[...] = jnp.zeros_like(out_ref)
    count = jnp.int32(0)
    for r in range(row_blocks):
        for c in range(2):
            kept = mask_ref[r, 2 * f_ref[0] + c]

            @pl.when(kept == 1)
            def _(r=r, c=c, count=count):
                total = own_ref[count] + other_ref[count].astype(
                    jnp.float32
                )
                out_ref[r * BLK : (r + 1) * BLK, c * BLK : (c + 1) * BLK] = (
                    total * scale
                ).astype(jnp.bfloat16)

            count = count + kept


def shape(dims, dtype=jnp.bfloat16):
    return jax.ShapeDtypeStruct(dims, dtype)


def cost(flops, size):
    return pl.CostEstimate(flops=flops, bytes_accessed=size, transcendentals=0)


def per_device(out_grad, live_rows, gate_pre, up_pre, down_weight, tile_mask):
    fsdp_count = lax.axis_size("fsdp")
    tensor_count = lax.axis_size("tensor")
    f = lax.axis_index("fsdp")
    t = lax.axis_index("tensor")
    ring_y = fsdp_count // 4
    ring_z = tensor_count // 2
    y, xh = f >> 2, (f >> 1) & 1
    xl = t >> (ring_z.bit_length() - 1)
    tok, width = out_grad.shape
    rows, units = gate_pre.shape
    scale = 1.0 / math.sqrt(rows * fsdp_count)
    f_arr = f.reshape(1).astype(jnp.int32)

    def over_f(x, move):
        return lax.ppermute(x, "fsdp", [(i, move(i)) for i in range(fsdp_count)])

    def over_t(x, move):
        return lax.ppermute(x, "tensor", [(i, move(i)) for i in range(tensor_count)])

    def y_step(x, d):
        return over_f(x, lambda i: (i + 4 * d) % fsdp_count)

    def swap_core(x):
        return over_f(x, lambda i: i ^ 1)

    def swap_xh(x):
        return over_f(x, lambda i: i ^ 2)

    def swap_xl(x):
        return over_t(x, lambda i: (i + ring_z) % tensor_count)

    grad_other = swap_xl(out_grad)
    live_other = swap_xl(live_rows)
    packed = pl.pallas_call(
        pack_kernel,
        out_shape=shape((CAP, BLK, BLK)),
        in_specs=[SMEM, SMEM, VMEM],
        out_specs=VMEM,
        name="pack",
        cost_estimate=cost(1000, 1 << 20),
    )(f_arr, tile_mask, down_weight)
    packed_other = swap_xh(packed)

    shard_count = fsdp_count // 2
    table, hidden = pl.pallas_call(
        table_kernel,
        out_shape=(shape((shard_count * TAB,), jnp.int32), shape((rows, units))),
        in_specs=[SMEM, SMEM, VMEM, VMEM],
        out_specs=(SMEM, VMEM),
        name="hidden",
        cost_estimate=cost(1000, 1 << 20),
    )(f_arr, tile_mask, gate_pre, up_pre)
    hidden_other = swap_core(hidden)

    def pair(own, other, index):
        first = (jnp.arange(2) == index).reshape((2,) + (1,) * own.ndim)
        return jnp.where(first, own[None], other[None])

    block = (2, tok, width)
    mine = lax.broadcasted_iota(jnp.int32, block, 0) == xl
    limit = jnp.where(mine, live_rows[0], live_other[0])
    masked = jnp.where(
        lax.broadcasted_iota(jnp.int32, block, 1) < limit,
        jnp.where(mine, out_grad[None], grad_other[None]),
        jnp.zeros((), jnp.bfloat16),
    )

    columns = [[k + 4 * i for i in range(ring_y)] for k in range(4)]
    chips = [
        [(2 * i + c) * tensor_count + half * ring_z + j for j in range(ring_z) for c in range(2)]
        for i in range(fsdp_count // 2)
        for half in range(2)
    ]
    panel = lax.all_gather(
        masked,
        ("fsdp", "tensor"),
        axis_index_groups=chips,
        tiled=True,
    ).reshape(2 * rows, width)
    core_arr = jnp.stack([f & 1, xh]).astype(jnp.int32)
    hidden_pair = pl.pallas_call(
        join_kernel,
        out_shape=shape((units, 2 * rows)),
        in_specs=[SMEM, VMEM, VMEM],
        out_specs=VMEM,
        name="join",
        cost_estimate=cost(1000, 1 << 20),
    )(core_arr, hidden, hidden_other)

    weights = jnp.zeros((ring_y, 2, CAP, BLK, BLK), jnp.bfloat16)

    def put(full, piece, at):
        return lax.dynamic_update_slice(full, piece[None], (at & (ring_y - 1), 0, 0, 0, 0))

    up = down = pair(packed, packed_other, xh)
    weights = put(weights, up, y)
    for d in range(1, ring_y // 2 + 1):
        up = y_step(up, 1)
        weights = put(weights, up, y - d + ring_y)
        if d < ring_y // 2:
            down = y_step(down, -1)
            weights = put(weights, down, y + d)
    weights = weights.reshape(shard_count, CAP, BLK, BLK)
    per_step = ring_y // 2

    panel_spec = pl.BlockSpec((2 * rows, width // ring_y * per_step), lambda i, tab, cr: (0, i))
    whole = pl.BlockSpec((units, 2 * rows), lambda i, tab, cr: (0, 0))
    tiles = pl.pallas_call(
        partial_kernel,
        out_shape=shape((ring_y, 2, CAP, BLK, BLK)),
        grid_spec=pltpu.PrefetchScalarGridSpec(
            num_scalar_prefetch=2,
            grid=(ring_y // per_step,),
            in_specs=[whole, panel_spec],
            out_specs=pl.BlockSpec(
                (per_step, 2, CAP, BLK, BLK), lambda i, tab, cr: (i, 0, 0, 0, 0)
            ),
        ),
        name="partial",
        cost_estimate=cost(ring_y * 16 * BLK * BLK * 2 * rows, ring_y << 19),
    )(table, core_arr, hidden_pair, panel)
    sums = lax.psum_scatter(
        tiles, "fsdp", scatter_dimension=0, axis_index_groups=columns, tiled=True
    )[0]
    own_sum, send_sum = sums[0].astype(jnp.float32), sums[1]
    other_sum = swap_xh(send_sum)

    groups = 4
    per_group = shard_count // groups
    acc_spec = pl.BlockSpec((rows, units), lambda i, tab, cr: (0, 0))
    panel_spec = pl.BlockSpec((2 * rows, width // groups), lambda i, tab, cr: (0, i))
    own_part, sent_part = pl.pallas_call(
        hidden_grad_kernel,
        out_shape=(shape((rows, units), jnp.float32), shape((rows, units), jnp.float32)),
        grid_spec=pltpu.PrefetchScalarGridSpec(
            num_scalar_prefetch=2,
            grid=(groups,),
            in_specs=[
                panel_spec,
                pl.BlockSpec((per_group, CAP, BLK, BLK), lambda i, tab, cr: (i, 0, 0, 0)),
            ],
            out_specs=(acc_spec, acc_spec),
            scratch_shapes=[pltpu.VMEM((2 * rows, units), jnp.float32)],
        ),
        name="hidden_grad",
        cost_estimate=cost(shard_count * CAP * 4 * rows * BLK * BLK, 6 << 20),
    )(table, core_arr, panel, weights)
    other_part = swap_core(sent_part)
    d_gate, d_up = pl.pallas_call(
        gates_kernel,
        out_shape=(shape((rows, units)), shape((rows, units))),
        in_specs=[VMEM] * 4,
        out_specs=(VMEM, VMEM),
        name="gates",
        compiler_params=pltpu.CompilerParams(vmem_limit_bytes=16 << 20),
        cost_estimate=cost(1000, 3 << 19),
    )(own_part, other_part, gate_pre, up_pre)
    d_weight = pl.pallas_call(
        functools.partial(place_kernel, scale),
        out_shape=shape(down_weight.shape),
        in_specs=[SMEM, SMEM, VMEM, VMEM],
        out_specs=VMEM,
        name="place",
        compiler_params=pltpu.CompilerParams(vmem_limit_bytes=16 << 20),
        cost_estimate=cost(1000, 1 << 20),
    )(f_arr, tile_mask, own_sum, other_sum)
    return (d_gate, d_up, d_weight)


def solution(mesh):
    return jax.shard_map(
        per_device,
        mesh=mesh,
        in_specs=(
            P(("fsdp", "tensor"), None),
            P(("fsdp", "tensor")),
            P("fsdp", "tensor"),
            P("fsdp", "tensor"),
            P("tensor", "fsdp"),
            P("tensor", None),
        ),
        out_specs=(P("fsdp", "tensor"), P("fsdp", "tensor"), P("tensor", "fsdp")),
        check_vma=False,
    )
```

```python
import functools
import math

import jax
import jax.numpy as jnp
from jax import lax
from jax.experimental import pallas as pl
from jax.experimental.pallas import tpu as pltpu
from jax.sharding import PartitionSpec as P


BLK = 128
CAP = 4
TAB = 8
TOK = 8


VMEM = pl.BlockSpec(memory_space=pltpu.VMEM)
SMEM = pl.BlockSpec(memory_space=pltpu.SMEM)


def by_ring(x):
    rows, width = x.shape
    return jnp.swapaxes(x.reshape(2, rows // (2 * TOK), TOK, width), 0, 1).reshape(rows, width)


def by_token(x):
    rows, width = x.shape
    return jnp.swapaxes(x.reshape(rows // (2 * TOK), 2, TOK, width), 0, 1).reshape(rows, width)


def mask_kernel(xl_ref, live_ref, live_other_ref, own_ref, other_ref, out_ref):
    rows = lax.broadcasted_iota(jnp.int32, own_ref.shape, 0)
    for at, live, ref in (
        (xl_ref[0], live_ref[0], own_ref),
        (1 - xl_ref[0], live_other_ref[0], other_ref),
    ):
        value = ref[...].astype(jnp.float32)
        out_ref[at] = jnp.where(rows < live, value, 0.0).astype(jnp.bfloat16)


def pack_kernel(f_ref, mask_ref, weight_ref, packed_ref):
    row_blocks = mask_ref.shape[0]
    packed_ref[...] = jnp.zeros_like(packed_ref)
    count = jnp.int32(0)
    for r in range(row_blocks):
        for c in range(2):
            kept = mask_ref[r, 2 * f_ref[0] + c]

            @pl.when(kept == 1)
            def _(r=r, c=c, count=count):
                packed_ref[count] = weight_ref[
                    r * BLK : (r + 1) * BLK, c * BLK : (c + 1) * BLK
                ]

            count = count + kept


def table_kernel(f_ref, mask_ref, gate_ref, up_ref, table_ref, hidden_ref):
    row_blocks = mask_ref.shape[0]
    core = lax.rem(f_ref[0], 2)

    def one_shard(s, carry):
        f = 2 * s + core
        base = s * TAB
        for k in range(TAB):
            table_ref[base + k] = 0
        count = jnp.int32(0)
        for r in range(row_blocks):
            for c in range(2):
                table_ref[base + count] = 2 * r + c
                count = count + mask_ref[r, 2 * f + c]
        return carry

    lax.fori_loop(0, table_ref.shape[0] // TAB, one_shard, 0)
    gate = gate_ref[...].astype(jnp.float32)
    up = up_ref[...].astype(jnp.float32)
    hidden = gate * jax.nn.sigmoid(gate) * up
    hidden_ref[...] = by_ring(hidden).astype(jnp.bfloat16)


def join_kernel(core_ref, own_ref, other_ref, out_ref):
    rows, _ = own_ref.shape
    first = core_ref[0] == 0
    pieces = []
    for at in range(0, rows, 2 * TOK):
        own = own_ref[at : at + 2 * TOK, :].astype(jnp.float32)
        other = other_ref[at : at + 2 * TOK, :].astype(jnp.float32)
        pieces += [jnp.where(first, own, other), jnp.where(first, other, own)]
    out_ref[...] = jnp.concatenate(pieces, axis=0).T.astype(jnp.bfloat16)


def partial_kernel(table_ref, core_ref, hidden_ref, panel_ref, out_ref):
    count = out_ref.shape[0]
    wide = 2 * BLK
    for i in range(count):
        dest = pl.program_id(0) * count + i
        for flip in range(2):
            xh = flip ^ core_ref[1]
            s = 2 * dest + xh
            at = pl.multiple_of(i * 4 * wide + (2 * xh + core_ref[0]) * wide, wide)
            right = panel_ref[:, pl.ds(at, wide)]
            places = [table_ref[s * TAB + k] for k in range(CAP)]
            rows = [pl.multiple_of((b >> 1) * BLK, BLK) for b in places]
            left = jnp.concatenate([hidden_ref[pl.ds(r, BLK), :] for r in rows], axis=0)
            term = jnp.dot(left, right, preferred_element_type=jnp.float32)
            for k, b in enumerate(places):
                tile = term[k * BLK : (k + 1) * BLK]
                kept = jnp.where((b & 1) == 0, tile[:, :BLK], tile[:, BLK:])
                out_ref[i, flip, k] = kept.astype(jnp.bfloat16)


def hidden_grad_kernel(
    table_ref, core_ref, panel_ref, weight_ref, own_ref, other_ref, sum_ref
):
    group = pl.program_id(0)
    shards = weight_ref.shape[0]
    wide = 2 * BLK
    rows = own_ref.shape[0]

    @pl.when(group == 0)
    def _():
        sum_ref[...] = jnp.zeros_like(sum_ref)

    for i in range(shards):
        s = group * shards + i
        at = pl.multiple_of((2 * i + core_ref[0]) * wide, wide)
        left = panel_ref[:, pl.ds(at, wide)]
        places = [table_ref[s * TAB + k] for k in range(CAP)]
        halves = []
        for k, b in enumerate(places):
            tile = weight_ref[i, k].astype(jnp.float32)
            second = (b & 1) == 1
            zero = jnp.zeros_like(tile)
            halves.append(
                jnp.concatenate(
                    [jnp.where(second, zero, tile), jnp.where(second, tile, zero)], axis=1
                ).astype(jnp.bfloat16)
            )
        term = lax.dot_general(
            left,
            jnp.concatenate(halves, axis=0),
            (((1,), (1,)), ((), ())),
            preferred_element_type=jnp.float32,
        )
        for k, b in enumerate(places):
            r = pl.multiple_of((b >> 1) * BLK, BLK)
            part = term[:, k * BLK : (k + 1) * BLK]
            sum_ref[:, pl.ds(r, BLK)] += part

    @pl.when(group == pl.num_programs(0) - 1)
    def _():
        first = core_ref[0] == 0
        for at in range(0, rows, 2 * TOK):
            a = sum_ref[2 * at : 2 * at + 2 * TOK, :]
            b = sum_ref[2 * at + 2 * TOK : 2 * at + 4 * TOK, :]
            own_ref[at : at + 2 * TOK, :] = jnp.where(first, a, b)
            other_ref[at : at + 2 * TOK, :] = jnp.where(first, b, a)


def gates_kernel(own_ref, other_ref, gate_ref, up_ref, d_gate_ref, d_up_ref):
    d_hidden = by_token(own_ref[...] + other_ref[...])
    gate = gate_ref[...].astype(jnp.float32)
    up = up_ref[...].astype(jnp.float32)
    s = jax.nn.sigmoid(gate)
    d_up_ref[...] = (d_hidden * gate * s).astype(jnp.bfloat16)
    d_gate_ref[...] = (d_hidden * up * s * (1.0 + gate * (1.0 - s))).astype(jnp.bfloat16)


def place_kernel(scale, f_ref, mask_ref, own_ref, other_ref, out_ref):
    row_blocks = mask_ref.shape[0]
    out_ref[...] = jnp.zeros_like(out_ref)
    count = jnp.int32(0)
    for r in range(row_blocks):
        for c in range(2):
            kept = mask_ref[r, 2 * f_ref[0] + c]

            @pl.when(kept == 1)
            def _(r=r, c=c, count=count):
                total = own_ref[count] + other_ref[count].astype(
                    jnp.float32
                )
                out_ref[r * BLK : (r + 1) * BLK, c * BLK : (c + 1) * BLK] = (
                    total * scale
                ).astype(jnp.bfloat16)

            count = count + kept


def shape(dims, dtype=jnp.bfloat16):
    return jax.ShapeDtypeStruct(dims, dtype)


def cost(flops, size):
    return pl.CostEstimate(flops=flops, bytes_accessed=size, transcendentals=0)


def per_device(out_grad, live_rows, gate_pre, up_pre, down_weight, tile_mask):
    fsdp_count = lax.axis_size("fsdp")
    tensor_count = lax.axis_size("tensor")
    f = lax.axis_index("fsdp")
    t = lax.axis_index("tensor")
    ring_y = fsdp_count // 4
    ring_z = tensor_count // 2
    y, xh = f >> 2, (f >> 1) & 1
    xl = t >> (ring_z.bit_length() - 1)
    tok, width = out_grad.shape
    rows, units = gate_pre.shape
    scale = 1.0 / math.sqrt(rows * fsdp_count)
    f_arr = f.reshape(1).astype(jnp.int32)

    def over_f(x, move):
        return lax.ppermute(x, "fsdp", [(i, move(i)) for i in range(fsdp_count)])

    def over_t(x, move):
        return lax.ppermute(x, "tensor", [(i, move(i)) for i in range(tensor_count)])

    def y_step(x, d):
        return over_f(x, lambda i: (i + 4 * d) % fsdp_count)

    def swap_core(x):
        return over_f(x, lambda i: i ^ 1)

    def swap_xh(x):
        return over_f(x, lambda i: i ^ 2)

    def swap_xl(x):
        return over_t(x, lambda i: (i + ring_z) % tensor_count)

    grad_other = swap_xl(out_grad)
    live_other = swap_xl(live_rows)
    packed = pl.pallas_call(
        pack_kernel,
        out_shape=shape((CAP, BLK, BLK)),
        in_specs=[SMEM, SMEM, VMEM],
        out_specs=VMEM,
        name="pack",
        cost_estimate=cost(1000, 1 << 20),
    )(f_arr, tile_mask, down_weight)
    packed_other = swap_xh(packed)

    shard_count = fsdp_count // 2
    table, hidden = pl.pallas_call(
        table_kernel,
        out_shape=(shape((shard_count * TAB,), jnp.int32), shape((rows, units))),
        in_specs=[SMEM, SMEM, VMEM, VMEM],
        out_specs=(SMEM, VMEM),
        name="hidden",
        cost_estimate=cost(1000, 1 << 20),
    )(f_arr, tile_mask, gate_pre, up_pre)
    hidden_other = swap_core(hidden)

    def pair(own, other, index):
        first = (jnp.arange(2) == index).reshape((2,) + (1,) * own.ndim)
        return jnp.where(first, own[None], other[None])

    masked = pl.pallas_call(
        mask_kernel,
        out_shape=shape((2, tok, width)),
        in_specs=[SMEM, SMEM, SMEM, VMEM, VMEM],
        out_specs=VMEM,
        name="mask",
        compiler_params=pltpu.CompilerParams(vmem_limit_bytes=16 << 20),
        cost_estimate=cost(1000, 1 << 20),
    )(xl.reshape(1).astype(jnp.int32), live_rows, live_other, out_grad, grad_other)

    columns = [[k + 4 * i for i in range(ring_y)] for k in range(4)]
    chips = [
        [(2 * i + c) * tensor_count + half * ring_z + j for j in range(ring_z) for c in range(2)]
        for i in range(fsdp_count // 2)
        for half in range(2)
    ]
    panel = lax.all_gather(
        masked,
        ("fsdp", "tensor"),
        axis_index_groups=chips,
        tiled=True,
    ).reshape(2 * rows, width)
    core_arr = jnp.stack([f & 1, xh]).astype(jnp.int32)
    hidden_pair = pl.pallas_call(
        join_kernel,
        out_shape=shape((units, 2 * rows)),
        in_specs=[SMEM, VMEM, VMEM],
        out_specs=VMEM,
        name="join",
        cost_estimate=cost(1000, 1 << 20),
    )(core_arr, hidden, hidden_other)

    weights = jnp.zeros((ring_y, 2, CAP, BLK, BLK), jnp.bfloat16)

    def put(full, piece, at):
        return lax.dynamic_update_slice(full, piece[None], (at & (ring_y - 1), 0, 0, 0, 0))

    up = down = pair(packed, packed_other, xh)
    weights = put(weights, up, y)
    for d in range(1, ring_y // 2 + 1):
        up = y_step(up, 1)
        weights = put(weights, up, y - d + ring_y)
        if d < ring_y // 2:
            down = y_step(down, -1)
            weights = put(weights, down, y + d)
    weights = weights.reshape(shard_count, CAP, BLK, BLK)
    per_step = ring_y // 2

    panel_spec = pl.BlockSpec((2 * rows, width // ring_y * per_step), lambda i, tab, cr: (0, i))
    whole = pl.BlockSpec((units, 2 * rows), lambda i, tab, cr: (0, 0))
    tiles = pl.pallas_call(
        partial_kernel,
        out_shape=shape((ring_y, 2, CAP, BLK, BLK)),
        grid_spec=pltpu.PrefetchScalarGridSpec(
            num_scalar_prefetch=2,
            grid=(ring_y // per_step,),
            in_specs=[whole, panel_spec],
            out_specs=pl.BlockSpec(
                (per_step, 2, CAP, BLK, BLK), lambda i, tab, cr: (i, 0, 0, 0, 0)
            ),
        ),
        name="partial",
        cost_estimate=cost(ring_y * 16 * BLK * BLK * 2 * rows, ring_y << 19),
    )(table, core_arr, hidden_pair, panel)
    sums = lax.psum_scatter(
        tiles, "fsdp", scatter_dimension=0, axis_index_groups=columns, tiled=True
    )[0]
    own_sum, send_sum = sums[0].astype(jnp.float32), sums[1]
    other_sum = swap_xh(send_sum)

    groups = 4
    per_group = shard_count // groups
    acc_spec = pl.BlockSpec((rows, units), lambda i, tab, cr: (0, 0))
    panel_spec = pl.BlockSpec((2 * rows, width // groups), lambda i, tab, cr: (0, i))
    own_part, sent_part = pl.pallas_call(
        hidden_grad_kernel,
        out_shape=(shape((rows, units), jnp.float32), shape((rows, units), jnp.float32)),
        grid_spec=pltpu.PrefetchScalarGridSpec(
            num_scalar_prefetch=2,
            grid=(groups,),
            in_specs=[
                panel_spec,
                pl.BlockSpec((per_group, CAP, BLK, BLK), lambda i, tab, cr: (i, 0, 0, 0)),
            ],
            out_specs=(acc_spec, acc_spec),
            scratch_shapes=[pltpu.VMEM((2 * rows, units), jnp.float32)],
        ),
        name="hidden_grad",
        cost_estimate=cost(shard_count * CAP * 4 * rows * BLK * BLK, 6 << 20),
    )(table, core_arr, panel, weights)
    other_part = swap_core(sent_part)
    d_gate, d_up = pl.pallas_call(
        gates_kernel,
        out_shape=(shape((rows, units)), shape((rows, units))),
        in_specs=[VMEM] * 4,
        out_specs=(VMEM, VMEM),
        name="gates",
        compiler_params=pltpu.CompilerParams(vmem_limit_bytes=16 << 20),
        cost_estimate=cost(1000, 3 << 19),
    )(own_part, other_part, gate_pre, up_pre)
    d_weight = pl.pallas_call(
        functools.partial(place_kernel, scale),
        out_shape=shape(down_weight.shape),
        in_specs=[SMEM, SMEM, VMEM, VMEM],
        out_specs=VMEM,
        name="place",
        compiler_params=pltpu.CompilerParams(vmem_limit_bytes=16 << 20),
        cost_estimate=cost(1000, 1 << 20),
    )(f_arr, tile_mask, own_sum, other_sum)
    return (d_gate, d_up, d_weight)


def solution(mesh):
    return jax.shard_map(
        per_device,
        mesh=mesh,
        in_specs=(
            P(("fsdp", "tensor"), None),
            P(("fsdp", "tensor")),
            P("fsdp", "tensor"),
            P("fsdp", "tensor"),
            P("tensor", "fsdp"),
            P("tensor", None),
        ),
        out_specs=(P("fsdp", "tensor"), P("fsdp", "tensor"), P("tensor", "fsdp")),
        check_vma=False,
    )
```

```python
import functools
import math

import jax
import jax.numpy as jnp
from jax import lax
from jax.experimental import pallas as pl
from jax.experimental.pallas import tpu as pltpu
from jax.sharding import PartitionSpec as P


BLK = 128
CAP = 4
TAB = 8
TOK = 8


VMEM = pl.BlockSpec(memory_space=pltpu.VMEM)
SMEM = pl.BlockSpec(memory_space=pltpu.SMEM)


def by_ring(x):
    rows, width = x.shape
    return jnp.swapaxes(x.reshape(2, rows // (2 * TOK), TOK, width), 0, 1).reshape(rows, width)


def by_token(x):
    rows, width = x.shape
    return jnp.swapaxes(x.reshape(rows // (2 * TOK), 2, TOK, width), 0, 1).reshape(rows, width)


def mask_kernel(xl_ref, live_ref, own_ref, other_ref, out_ref):
    rows = lax.broadcasted_iota(jnp.int32, other_ref.shape, 0)
    value = other_ref[...].astype(jnp.float32)
    out_ref[xl_ref[0]] = own_ref[...]
    out_ref[1 - xl_ref[0]] = jnp.where(rows < live_ref[0], value, 0.0).astype(jnp.bfloat16)


def pack_kernel(f_ref, mask_ref, weight_ref, packed_ref):
    row_blocks = mask_ref.shape[0]
    packed_ref[...] = jnp.zeros_like(packed_ref)
    count = jnp.int32(0)
    for r in range(row_blocks):
        for c in range(2):
            kept = mask_ref[r, 2 * f_ref[0] + c]

            @pl.when(kept == 1)
            def _(r=r, c=c, count=count):
                packed_ref[count] = weight_ref[
                    r * BLK : (r + 1) * BLK, c * BLK : (c + 1) * BLK
                ]

            count = count + kept


def table_kernel(f_ref, mask_ref, gate_ref, up_ref, table_ref, hidden_ref):
    row_blocks = mask_ref.shape[0]
    core = lax.rem(f_ref[0], 2)

    def one_shard(s, carry):
        f = 2 * s + core
        base = s * TAB
        for k in range(TAB):
            table_ref[base + k] = 0
        count = jnp.int32(0)
        for r in range(row_blocks):
            for c in range(2):
                table_ref[base + count] = 2 * r + c
                count = count + mask_ref[r, 2 * f + c]
        return carry

    lax.fori_loop(0, table_ref.shape[0] // TAB, one_shard, 0)
    gate = gate_ref[...].astype(jnp.float32)
    up = up_ref[...].astype(jnp.float32)
    hidden = gate * jax.nn.sigmoid(gate) * up
    hidden_ref[...] = by_ring(hidden).astype(jnp.bfloat16)


def join_kernel(core_ref, own_ref, other_ref, out_ref):
    rows, _ = own_ref.shape
    first = core_ref[0] == 0
    pieces = []
    for at in range(0, rows, 2 * TOK):
        own = own_ref[at : at + 2 * TOK, :].astype(jnp.float32)
        other = other_ref[at : at + 2 * TOK, :].astype(jnp.float32)
        pieces += [jnp.where(first, own, other), jnp.where(first, other, own)]
    out_ref[...] = jnp.concatenate(pieces, axis=0).T.astype(jnp.bfloat16)


def partial_kernel(table_ref, core_ref, hidden_ref, panel_ref, out_ref):
    count = out_ref.shape[0]
    wide = 2 * BLK
    for i in range(count):
        dest = pl.program_id(0) * count + i
        for flip in range(2):
            xh = flip ^ core_ref[1]
            s = 2 * dest + xh
            at = pl.multiple_of(i * 4 * wide + (2 * xh + core_ref[0]) * wide, wide)
            right = panel_ref[:, pl.ds(at, wide)]
            places = [table_ref[s * TAB + k] for k in range(CAP)]
            rows = [pl.multiple_of((b >> 1) * BLK, BLK) for b in places]
            left = jnp.concatenate([hidden_ref[pl.ds(r, BLK), :] for r in rows], axis=0)
            term = jnp.dot(left, right, preferred_element_type=jnp.float32)
            for k, b in enumerate(places):
                tile = term[k * BLK : (k + 1) * BLK]
                kept = jnp.where((b & 1) == 0, tile[:, :BLK], tile[:, BLK:])
                out_ref[i, flip, k] = kept.astype(jnp.bfloat16)


def hidden_grad_kernel(
    table_ref, core_ref, panel_ref, weight_ref, own_ref, other_ref, sum_ref
):
    group = pl.program_id(0)
    shards = weight_ref.shape[0]
    wide = 2 * BLK
    rows = own_ref.shape[0]

    @pl.when(group == 0)
    def _():
        sum_ref[...] = jnp.zeros_like(sum_ref)

    for i in range(shards):
        s = group * shards + i
        at = pl.multiple_of((2 * i + core_ref[0]) * wide, wide)
        left = panel_ref[:, pl.ds(at, wide)]
        places = [table_ref[s * TAB + k] for k in range(CAP)]
        halves = []
        for k, b in enumerate(places):
            tile = weight_ref[i, k].astype(jnp.float32)
            second = (b & 1) == 1
            zero = jnp.zeros_like(tile)
            halves.append(
                jnp.concatenate(
                    [jnp.where(second, zero, tile), jnp.where(second, tile, zero)], axis=1
                ).astype(jnp.bfloat16)
            )
        term = lax.dot_general(
            left,
            jnp.concatenate(halves, axis=0),
            (((1,), (1,)), ((), ())),
            preferred_element_type=jnp.float32,
        )
        for k, b in enumerate(places):
            r = pl.multiple_of((b >> 1) * BLK, BLK)
            part = term[:, k * BLK : (k + 1) * BLK]
            sum_ref[:, pl.ds(r, BLK)] += part

    @pl.when(group == pl.num_programs(0) - 1)
    def _():
        first = core_ref[0] == 0
        for at in range(0, rows, 2 * TOK):
            a = sum_ref[2 * at : 2 * at + 2 * TOK, :]
            b = sum_ref[2 * at + 2 * TOK : 2 * at + 4 * TOK, :]
            own_ref[at : at + 2 * TOK, :] = jnp.where(first, a, b)
            other_ref[at : at + 2 * TOK, :] = jnp.where(first, b, a)


def gates_kernel(own_ref, other_ref, gate_ref, up_ref, d_gate_ref, d_up_ref):
    d_hidden = by_token(own_ref[...] + other_ref[...])
    gate = gate_ref[...].astype(jnp.float32)
    up = up_ref[...].astype(jnp.float32)
    s = jax.nn.sigmoid(gate)
    d_up_ref[...] = (d_hidden * gate * s).astype(jnp.bfloat16)
    d_gate_ref[...] = (d_hidden * up * s * (1.0 + gate * (1.0 - s))).astype(jnp.bfloat16)


def place_kernel(scale, f_ref, mask_ref, own_ref, other_ref, out_ref):
    row_blocks = mask_ref.shape[0]
    out_ref[...] = jnp.zeros_like(out_ref)
    count = jnp.int32(0)
    for r in range(row_blocks):
        for c in range(2):
            kept = mask_ref[r, 2 * f_ref[0] + c]

            @pl.when(kept == 1)
            def _(r=r, c=c, count=count):
                total = own_ref[count] + other_ref[count].astype(
                    jnp.float32
                )
                out_ref[r * BLK : (r + 1) * BLK, c * BLK : (c + 1) * BLK] = (
                    total * scale
                ).astype(jnp.bfloat16)

            count = count + kept


def shape(dims, dtype=jnp.bfloat16):
    return jax.ShapeDtypeStruct(dims, dtype)


def cost(flops, size):
    return pl.CostEstimate(flops=flops, bytes_accessed=size, transcendentals=0)


def per_device(out_grad, live_rows, gate_pre, up_pre, down_weight, tile_mask):
    fsdp_count = lax.axis_size("fsdp")
    tensor_count = lax.axis_size("tensor")
    f = lax.axis_index("fsdp")
    t = lax.axis_index("tensor")
    ring_y = fsdp_count // 4
    ring_z = tensor_count // 2
    y, xh = f >> 2, (f >> 1) & 1
    xl = t >> (ring_z.bit_length() - 1)
    tok, width = out_grad.shape
    rows, units = gate_pre.shape
    scale = 1.0 / math.sqrt(rows * fsdp_count)
    f_arr = f.reshape(1).astype(jnp.int32)

    def over_f(x, move):
        return lax.ppermute(x, "fsdp", [(i, move(i)) for i in range(fsdp_count)])

    def over_t(x, move):
        return lax.ppermute(x, "tensor", [(i, move(i)) for i in range(tensor_count)])

    def y_step(x, d):
        return over_f(x, lambda i: (i + 4 * d) % fsdp_count)

    def swap_core(x):
        return over_f(x, lambda i: i ^ 1)

    def swap_xh(x):
        return over_f(x, lambda i: i ^ 2)

    def swap_xl(x):
        return over_t(x, lambda i: (i + ring_z) % tensor_count)

    grad_other = swap_xl(out_grad)
    live_other = swap_xl(live_rows)
    packed = pl.pallas_call(
        pack_kernel,
        out_shape=shape((CAP, BLK, BLK)),
        in_specs=[SMEM, SMEM, VMEM],
        out_specs=VMEM,
        name="pack",
        cost_estimate=cost(1000, 1 << 20),
    )(f_arr, tile_mask, down_weight)
    packed_other = swap_xh(packed)

    shard_count = fsdp_count // 2
    table, hidden = pl.pallas_call(
        table_kernel,
        out_shape=(shape((shard_count * TAB,), jnp.int32), shape((rows, units))),
        in_specs=[SMEM, SMEM, VMEM, VMEM],
        out_specs=(SMEM, VMEM),
        name="hidden",
        cost_estimate=cost(1000, 1 << 20),
    )(f_arr, tile_mask, gate_pre, up_pre)
    hidden_other = swap_core(hidden)

    def pair(own, other, index):
        first = (jnp.arange(2) == index).reshape((2,) + (1,) * own.ndim)
        return jnp.where(first, own[None], other[None])

    own_masked = jnp.where(
        jnp.arange(tok)[:, None] < live_rows[0], out_grad, jnp.zeros((), jnp.bfloat16)
    )
    masked = pl.pallas_call(
        mask_kernel,
        out_shape=shape((2, tok, width)),
        in_specs=[SMEM, SMEM, VMEM, VMEM],
        out_specs=VMEM,
        name="mask",
        compiler_params=pltpu.CompilerParams(vmem_limit_bytes=16 << 20),
        cost_estimate=cost(1000, 1 << 20),
    )(xl.reshape(1).astype(jnp.int32), live_other, own_masked, grad_other)

    columns = [[k + 4 * i for i in range(ring_y)] for k in range(4)]
    chips = [
        [(2 * i + c) * tensor_count + half * ring_z + j for j in range(ring_z) for c in range(2)]
        for i in range(fsdp_count // 2)
        for half in range(2)
    ]
    panel = lax.all_gather(
        masked,
        ("fsdp", "tensor"),
        axis_index_groups=chips,
        tiled=True,
    ).reshape(2 * rows, width)
    core_arr = jnp.stack([f & 1, xh]).astype(jnp.int32)
    hidden_pair = pl.pallas_call(
        join_kernel,
        out_shape=shape((units, 2 * rows)),
        in_specs=[SMEM, VMEM, VMEM],
        out_specs=VMEM,
        name="join",
        compiler_params=pltpu.CompilerParams(vmem_limit_bytes=16 << 20),
        cost_estimate=cost(1000, 1 << 20),
    )(core_arr, hidden, hidden_other)

    weights = jnp.zeros((ring_y, 2, CAP, BLK, BLK), jnp.bfloat16)

    def put(full, piece, at):
        return lax.dynamic_update_slice(full, piece[None], (at & (ring_y - 1), 0, 0, 0, 0))

    up = down = pair(packed, packed_other, xh)
    weights = put(weights, up, y)
    for d in range(1, ring_y // 2 + 1):
        up = y_step(up, 1)
        weights = put(weights, up, y - d + ring_y)
        if d < ring_y // 2:
            down = y_step(down, -1)
            weights = put(weights, down, y + d)
    weights = weights.reshape(shard_count, CAP, BLK, BLK)
    per_step = ring_y // 2

    panel_spec = pl.BlockSpec((2 * rows, width // ring_y * per_step), lambda i, tab, cr: (0, i))
    whole = pl.BlockSpec((units, 2 * rows), lambda i, tab, cr: (0, 0))
    tiles = pl.pallas_call(
        partial_kernel,
        out_shape=shape((ring_y, 2, CAP, BLK, BLK)),
        grid_spec=pltpu.PrefetchScalarGridSpec(
            num_scalar_prefetch=2,
            grid=(ring_y // per_step,),
            in_specs=[whole, panel_spec],
            out_specs=pl.BlockSpec(
                (per_step, 2, CAP, BLK, BLK), lambda i, tab, cr: (i, 0, 0, 0, 0)
            ),
        ),
        name="partial",
        compiler_params=pltpu.CompilerParams(vmem_limit_bytes=20 << 20),
        cost_estimate=cost(ring_y * 16 * BLK * BLK * 2 * rows, ring_y << 19),
    )(table, core_arr, hidden_pair, panel)
    sums = lax.psum_scatter(
        tiles, "fsdp", scatter_dimension=0, axis_index_groups=columns, tiled=True
    )[0]
    sums, send_sum = lax.optimization_barrier((sums, sums[1]))
    own_sum = sums[0].astype(jnp.float32)
    other_sum = swap_xh(send_sum)

    groups = 4
    per_group = shard_count // groups
    acc_spec = pl.BlockSpec((rows, units), lambda i, tab, cr: (0, 0))
    panel_spec = pl.BlockSpec((2 * rows, width // groups), lambda i, tab, cr: (0, i))
    own_part, sent_part = pl.pallas_call(
        hidden_grad_kernel,
        out_shape=(shape((rows, units), jnp.float32), shape((rows, units), jnp.float32)),
        grid_spec=pltpu.PrefetchScalarGridSpec(
            num_scalar_prefetch=2,
            grid=(groups,),
            in_specs=[
                panel_spec,
                pl.BlockSpec((per_group, CAP, BLK, BLK), lambda i, tab, cr: (i, 0, 0, 0)),
            ],
            out_specs=(acc_spec, acc_spec),
            scratch_shapes=[pltpu.VMEM((2 * rows, units), jnp.float32)],
        ),
        name="hidden_grad",
        cost_estimate=cost(shard_count * CAP * 4 * rows * BLK * BLK, 6 << 20),
    )(table, core_arr, panel, weights)
    other_part = swap_core(sent_part)
    d_gate, d_up = pl.pallas_call(
        gates_kernel,
        out_shape=(shape((rows, units)), shape((rows, units))),
        in_specs=[VMEM] * 4,
        out_specs=(VMEM, VMEM),
        name="gates",
        compiler_params=pltpu.CompilerParams(vmem_limit_bytes=16 << 20),
        cost_estimate=cost(1000, 3 << 19),
    )(own_part, other_part, gate_pre, up_pre)
    d_weight = pl.pallas_call(
        functools.partial(place_kernel, scale),
        out_shape=shape(down_weight.shape),
        in_specs=[SMEM, SMEM, VMEM, VMEM],
        out_specs=VMEM,
        name="place",
        compiler_params=pltpu.CompilerParams(vmem_limit_bytes=16 << 20),
        cost_estimate=cost(1000, 1 << 20),
    )(f_arr, tile_mask, own_sum, other_sum)
    return (d_gate, d_up, d_weight)


def solution(mesh):
    return jax.shard_map(
        per_device,
        mesh=mesh,
        in_specs=(
            P(("fsdp", "tensor"), None),
            P(("fsdp", "tensor")),
            P("fsdp", "tensor"),
            P("fsdp", "tensor"),
            P("tensor", "fsdp"),
            P("tensor", None),
        ),
        out_specs=(P("fsdp", "tensor"), P("fsdp", "tensor"), P("tensor", "fsdp")),
        check_vma=False,
    )
```
